32 devices in a mesh: sx: 4 (over x, core), sy: 2 (over y), cr: 4 (over z).
Axes of the slice: x: 2, y: 2, z: 4, core: 2. Of those that a mesh axis runs over, the one named last changes fastest.
Arguments:
- adjoint: float32 [256, 64, 256], P('cr', 'sx', 'sy'), may hold values from -6 to 6
- sensor_rows: bfloat16 [3072, 64, 256], P('cr', 'sx', 'sy'), may hold values from -0.046875 to 0.046875
- cell_ids: int32 [64, 256], P('sx', 'sy'), may hold values from 0 to 15
- mat_diag: float32 [16], replicated, may hold values from -0.15 to 0.15
- mat_cond: float32 [16], replicated, may hold values from 0.2 to 0.45
- cheb_coef: float32 [9], replicated, may hold values from 0.3 to 1
Outputs:
- smoothed: float32 [256, 64, 256], P('cr', 'sx', 'sy')
- panel: float32 [3072, 256], P('cr', ('sx', 'sy'))
The draws below stay inside these ranges and needn't reach their ends.
All inputs are finite; a program needn't handle non-finite values.
Results may differ from the reference program's by a relative error of at most 0.0029.
Values may be sent and summed in bfloat16 or wider, within the bound.
No kernel may reach another device: no remote copies, remote signals or barrier semaphores. Data moves between devices by JAX's collectives and lax.ppermute only.
A program may use at most 64 MiB of HBM per device.

```python
import jax
import jax.numpy as jnp
from jax import lax

COLS = 256
DEG = 8
NMAT = 16
ROWS = 3072
NX = 64
NY = 256


def plant(drawn, own_key, least, largest):
    longest = drawn.shape.index(max(drawn.shape))
    spots = []
    for shift in (0, 1):
        where = [jax.random.randint(jax.random.fold_in(own_key, axis), (), 0, length) for axis, length in enumerate(drawn.shape)]
        where[longest] = (where[longest] + shift) % drawn.shape[longest]
        spots.append(tuple(where))
    return drawn.at[spots[0]].set(least).at[spots[1]].set(largest)


def levels(stream_key, extent, pieces, smallest, top_value):
    gain, own = 1.0, jax.random.fold_in(stream_key, 6)
    for position, shards_of in pieces:
        steps = jnp.exp(jax.random.uniform(jax.random.fold_in(own, position), (shards_of,), jnp.float32, smallest / len(pieces), top_value / len(pieces)))
        gain = gain * jnp.repeat(steps, extent[position] // shards_of).reshape([-1 if axis == position else 1 for axis in range(len(extent))])
    return gain


def gaussian(rng, dims, spread, reach, shards=(), held_as=jnp.bfloat16):
    drawn = jax.random.normal(rng, dims, jnp.float32) * spread
    if len(shards) > 0:
        drawn = levels(rng, dims, shards, -0.22, 0.18) * drawn
    return jnp.clip(drawn, min=-reach, max=reach).astype(held_as)


def setup_inputs(seed: int = 0) -> dict:
    seeds = jax.random.split(jax.random.key(seed), 7)
    return {
        "adjoint": gaussian(seeds[0], (COLS, NX, NY), 1.0, 6.0, ((0, 4), (1, 4), (2, 2)), jnp.float32),
        "sensor_rows": gaussian(seeds[1], (ROWS, NX, NY), (NX * NY) ** -0.5, 0.046875, ((0, 4), (1, 4), (2, 2))),
        "cell_ids": plant(jax.random.randint(seeds[2], (NX, NY), 0, NMAT), jax.random.fold_in(seeds[2], 1), 0, NMAT - 1).astype(jnp.int32),
        "mat_diag": jnp.clip(jax.random.uniform(seeds[3], (NMAT,), jnp.float32, -0.15, 0.15), -0.15, 0.15),
        "mat_cond": jnp.clip(jax.random.uniform(seeds[4], (NMAT,), jnp.float32, 0.2, 0.45), 0.2, 0.45),
        "cheb_coef": jnp.clip(jax.random.uniform(seeds[5], (DEG + 1,), jnp.float32, 0.3, 1.0), 0.3, 1.0),
    }


def apply_scaled(field, diag, cond):
    weighted = cond * field
    padded = jnp.pad(weighted, ((0, 0), (1, 1), (1, 1)))
    beside = padded[:, :-2, 1:-1] + padded[:, 2:, 1:-1]
    beside = beside + padded[:, 1:-1, :-2] + padded[:, 1:-1, 2:]
    return diag * field + cond * beside


def reference(adjoint, sensor_rows, cell_ids, mat_diag, mat_cond, cheb_coef):
    diag = mat_diag[cell_ids]
    cond = mat_cond[cell_ids]
    older = adjoint
    current = apply_scaled(adjoint, diag, cond)
    smoothed = cheb_coef[0] * adjoint + cheb_coef[1] * current
    for order in range(2, DEG + 1):
        newer = 2.0 * apply_scaled(current, diag, cond) - older
        older = current
        current = newer
        smoothed = smoothed + cheb_coef[order] * newer
    lowered = smoothed.astype(jnp.bfloat16)
    flat_rows = sensor_rows.reshape(sensor_rows.shape[0], -1)
    flat_cols = lowered.reshape(lowered.shape[0], -1)
    panel = lax.dot_general(flat_rows, flat_cols, (((1,), (1,)), ((), ())), preferred_element_type=jnp.float32)
    return smoothed, panel
```

```python
import functools

import jax
import jax.numpy as jnp
from jax import lax
from jax.experimental import pallas as pl
from jax.experimental.pallas import tpu as pltpu
from jax.sharding import PartitionSpec as P

DEG = 8
SUB = 8
LANES = 128
SIDE = 2 * DEG
F32 = jnp.float32
BF16 = jnp.bfloat16


def partner(i, odd, size):
    j = i ^ 1 if not odd else ((i + 1) ^ 1) - 1
    return j if 0 <= j < size else None


def pairing(kind_x, kind_y, size_x, size_y):
    pairs = []
    for i in range(size_x):
        for j in range(size_y):
            a = i if kind_x is None else partner(i, kind_x, size_x)
            b = j if kind_y is None else partner(j, kind_y, size_y)
            if a is not None and b is not None:
                pairs.append((i * size_y + j, a * size_y + b))
    return pairs


def edge_lanes():
    place = lax.broadcasted_iota(jnp.int32, (SUB, LANES), 1) & (SIDE - 1)
    return jnp.where(place < DEG, DEG - 1 - place, LANES - 1 + DEG - place)


def lane_gather(tile, index):
    return jnp.take_along_axis(tile, index, axis=1, mode="promise_in_bounds")


def pack_kernel(groups, width_x, n_edge, flags, adj_ref, ids_ref, *out_refs):
    row_refs = out_refs[:2]
    strip_refs = out_refs[2:]
    ids = ids_ref[...].astype(F32) + 1.0
    for which in range(2):
        upper = flags[0] if which == 0 else 1 - flags[0]
        base = jnp.where(upper == 1, width_x - DEG, 0)
        base = pl.multiple_of(base, SUB)

        for row in range(DEG):
            for g in range(groups):
                row_refs[which][row * groups + g] = adj_ref[pl.ds(g * SUB * width_x + base + row, SUB, stride=width_x), :]
        row_refs[which][DEG * groups] = ids_ref[pl.ds(base, SUB), :].astype(F32) + 1.0
    index = edge_lanes()
    lane = lax.broadcasted_iota(jnp.int32, (SUB, LANES), 1)
    low_side = (lane & (SIDE - 1)) < DEG
    n_kinds = len(strip_refs) // 3
    for row in range(width_x):
        strip = jnp.zeros((SUB, LANES), F32)
        for g in range(groups):
            tile = adj_ref[pl.ds(g * SUB * width_x + row, SUB, stride=width_x), :]
            strip = jnp.where((lane // SIDE) == g, lane_gather(tile, index), strip)
        for kind in range(n_kinds):
            upper = flags[1] if kind == 0 else 1 - flags[1]
            keep = jnp.where(low_side, 1 - upper, upper) == 1
            strip_refs[3 * kind][row] = jnp.where(keep, strip, 0.0)
    for tile_x in range(width_x // SUB):
        strip = lane_gather(ids[tile_x * SUB : (tile_x + 1) * SUB], index)
        for kind in range(n_kinds):
            upper = flags[1] if kind == 0 else 1 - flags[1]
            keep = jnp.where(low_side, 1 - upper, upper) == 1
            strip_refs[3 * kind][width_x + tile_x] = jnp.where(keep, strip, 0.0)
    for kind in range(n_kinds):
        for which in range(2):
            upper = flags[0] if which == 0 else 1 - flags[0]
            base = jnp.where(upper == 1, width_x - DEG, 0)
            tile_base = jnp.where(upper == 1, width_x // SUB - 1, 0)
            for row in range(DEG):
                strip_refs[3 * kind + 1 + which][row] = strip_refs[3 * kind][base + row]
            strip_refs[3 * kind + 1 + which][DEG] = strip_refs[3 * kind][width_x + tile_base]


def filter_kernel(
    groups, width_x, flags, diag_ref, cond_ref, coef_ref, adj_ref, ids_ref, even_ref, odd_ref, strip_ref, strip_even_ref,
    strip_odd_ref, smooth_ref, low_ref, u_ref, a_ref, b_ref, c2_ref, d2_ref, c2s_ref, d2s_ref, cond_t, ratio_t, inv_t,
):
    tall = width_x + 2 * DEG
    n_mat = diag_ref.shape[0]
    lane = lax.broadcasted_iota(jnp.int32, (SUB, LANES), 1)
    is_even = flags[0] == 1

    def lookup(ids):
        diag = jnp.zeros_like(ids)
        cond = jnp.zeros_like(ids)
        for m in range(n_mat):
            hit = ids == float(m + 1)
            diag = jnp.where(hit, diag_ref[m], diag)
            cond = jnp.where(hit, cond_ref[m], cond)
        return diag, cond

    def spread(row_tile, x0, c_ref, d_ref, own):
        diag, cond = lookup(row_tile)
        for s in range(SUB):
            c_row = jnp.broadcast_to(cond[s : s + 1], (SUB, LANES))
            d_row = jnp.broadcast_to(diag[s : s + 1], (SUB, LANES))
            c_ref[x0 + s] = 2.0 * c_row * c_row
            d_ref[x0 + s] = 2.0 * d_row
            if own:
                inverse = 1.0 / c_row
                cond_t[x0 + s - DEG] = c_row
                inv_t[x0 + s - DEG] = inverse
                ratio_t[x0 + s - DEG] = d_row * inverse
        return cond

    def scaled(tiles, cond_row):
        return tiles * jnp.broadcast_to(cond_row, (SUB, LANES))

    repeat = lane & (SIDE - 1)
    for high in (False, True):
        x0 = tall - DEG if high else 0
        from_even = is_even if high else jnp.logical_not(is_even)
        ids = jnp.where(from_even, even_ref[DEG * groups], odd_ref[DEG * groups])
        cond = spread(ids, x0, c2_ref, d2_ref, False)
        ids_s = jnp.where(from_even, strip_even_ref[DEG], strip_odd_ref[DEG])
        cond_s = spread(lane_gather(ids_s, repeat), x0, c2s_ref, d2s_ref, False)
        for row in range(DEG):
            for g in range(groups):
                tile = jnp.where(from_even, even_ref[row * groups + g], odd_ref[row * groups + g])
                u_ref[x0 + row, g] = scaled(tile, cond[row : row + 1])
            tile = jnp.where(from_even, strip_even_ref[row], strip_odd_ref[row])
            u_ref[x0 + row, groups] = scaled(tile, cond_s[row : row + 1])
    for tile_x in range(width_x // SUB):
        x0 = DEG + tile_x * SUB
        cond = spread(ids_ref[tile_x * SUB : (tile_x + 1) * SUB, :].astype(F32) + 1.0, x0, c2_ref, d2_ref, True)
        cond_s = spread(lane_gather(strip_ref[width_x + tile_x], repeat), x0, c2s_ref, d2s_ref, False)
        for row in range(SUB):
            for g in range(groups):
                tile = adj_ref[pl.ds(g * SUB * width_x + tile_x * SUB + row, SUB, stride=width_x), :]
                u_ref[x0 + row, g] = scaled(tile, cond[row : row + 1])
            u_ref[x0 + row, groups] = scaled(strip_ref[tile_x * SUB + row], cond_s[row : row + 1])

    first_lane = lane == 0
    last_lane = lane == LANES - 1
    place = lane & (SIDE - 1)
    at_high = place == DEG - 1
    at_low = place == DEG
    junction = lane // SIDE

    def across(tiles, strip):
        sums = []
        meet = None
        for g, tile in enumerate(tiles):
            off = g * SIDE + DEG
            edge = pltpu.roll(strip, LANES - off, 1)
            left = jnp.where(first_lane, edge, pltpu.roll(tile, 1, 1))
            right = jnp.where(last_lane, edge, pltpu.roll(tile, LANES - 1, 1))
            sums.append(left + right)
            moved = pltpu.roll(tile, off, 1)
            meet = moved if meet is None else jnp.where(junction == g, moved, meet)
        up = jnp.where(at_high, meet, pltpu.roll(strip, LANES - 1, 1))
        down = jnp.where(at_low, meet, pltpu.roll(strip, 1, 1))
        return sums, up + down

    def neighbours(src, x, with_strip):
        tiles = [src[x, g] for g in range(groups)]
        strip = src[x, groups]
        sums, strip_sum = across(tiles, strip)
        sums = [s + (src[x - 1, g] + src[x + 1, g]) for g, s in enumerate(sums)]
        if with_strip:
            strip_sum = strip_sum + (src[x - 1, groups] + src[x + 1, groups])
        return tiles, strip, sums, strip_sum

    top = coef_ref[DEG]
    for order in range(DEG - 1, 0, -1):
        lo = DEG - order
        src = u_ref if order == DEG - 1 else (a_ref if (order % 2 == 0) else b_ref)
        dst = b_ref if (order % 2 == 0) else a_ref
        coef = coef_ref[order]

        def step(x, carry, order=order, src=src, dst=dst, coef=coef):
            tiles, strip, sums, strip_sum = neighbours(src, x, True)
            c2 = c2_ref[x]
            d2 = d2_ref[x]
            c2s = c2s_ref[x]
            d2s = d2s_ref[x]
            for g in range(groups + 1):
                tile, total = (tiles[g], sums[g]) if g < groups else (strip, strip_sum)
                cc, dd = (c2, d2) if g < groups else (c2s, d2s)
                applied = dd * tile + cc * total
                if order == DEG - 1:
                    value = coef * tile + top * applied
                elif order == DEG - 2:
                    value = (coef - top) * u_ref[x, g] + applied
                else:
                    value = coef * u_ref[x, g] + (applied - dst[x, g])
                dst[x, g] = value
            return carry

        lax.fori_loop(lo, tall - lo, step, 0)
    first = a_ref
    second = b_ref

    def last(i, carry):
        x = i + DEG
        tiles, _, sums, _ = neighbours(first, x, False)
        cond = cond_t[i]
        ratio = ratio_t[i]
        inverse = inv_t[i]
        out = []
        for g in range(groups):
            start = coef_ref[0] * u_ref[x, g] - second[x, g]
            value = inverse * start + (ratio * tiles[g] + cond * sums[g])
            smooth_ref[pl.ds(g * SUB * width_x + i, SUB, stride=width_x), :] = value
            out.append(value)
        column = pl.multiple_of(i * LANES, LANES)
        for g in range(0, groups, 2):
            both = jnp.concatenate(out[g : g + 2], axis=0)
            low_ref[pl.ds(g * SUB, 2 * SUB), pl.ds(column, LANES)] = both.astype(BF16)
        return carry

    lax.fori_loop(0, width_x, last, 0)


def vmem():
    return pl.BlockSpec(memory_space=pltpu.VMEM)


def smem():
    return pl.BlockSpec(memory_space=pltpu.SMEM)


def filtered(adjoint, cell_ids, mat_diag, mat_cond, cheb_coef):
    cols, width_x, width_y = adjoint.shape
    groups = cols // SUB
    assert width_y == LANES and width_x % SUB == 0 and width_x >= DEG
    assert cols % SIDE == 0 and groups * SIDE <= LANES
    size_x = lax.axis_size("sx")
    size_y = lax.axis_size("sy")
    even_x = 1 - lax.axis_index("sx") % 2
    even_y = 1 - lax.axis_index("sy") % 2
    flags = jnp.stack([even_x, even_y]).astype(jnp.int32)
    flat = adjoint.reshape(cols * width_x, width_y)
    n_kinds = 2 if size_y > 2 else 1
    row_shape = jax.ShapeDtypeStruct((DEG * groups + 1, SUB, LANES), F32)
    strip_shape = jax.ShapeDtypeStruct((width_x + width_x // SUB, SUB, LANES), F32)
    corner_shape = jax.ShapeDtypeStruct((DEG + 1, SUB, LANES), F32)
    packed = pl.pallas_call(
        functools.partial(pack_kernel, groups, width_x, n_kinds),
        out_shape=[row_shape] * 2 + [strip_shape, corner_shape, corner_shape] * n_kinds,
        in_specs=[smem(), vmem(), vmem()],
        out_specs=[vmem()] * (2 + 3 * n_kinds),
        name="pack",
    )(flags, flat, cell_ids)

    def swap(value, kind_x, kind_y):
        pairs = pairing(kind_x, kind_y, size_x, size_y)
        if not pairs:
            return jnp.zeros_like(value)
        return lax.ppermute(value, ("sx", "sy"), pairs)

    odd = swap(packed[1], 1, None)
    even = swap(packed[0], 0, None)
    strips = []
    for kind in range(n_kinds):
        strips.append(
            (
                swap(packed[2 + 3 * kind], None, kind),
                swap(packed[3 + 3 * kind], 0, kind),
                swap(packed[4 + 3 * kind], 1, kind),
            )
        )
    strip, strip_even, strip_odd = (functools.reduce(jnp.add, part) for part in zip(*strips))
    tall = width_x + 2 * DEG
    table = pltpu.VMEM((tall, SUB, LANES), F32)
    own_table = pltpu.VMEM((width_x, SUB, LANES), F32)
    field = pltpu.VMEM((tall, groups + 1, SUB, LANES), F32)
    smooth, low = pl.pallas_call(
        functools.partial(filter_kernel, groups, width_x),
        out_shape=[
            jax.ShapeDtypeStruct((cols * width_x, width_y), F32),
            jax.ShapeDtypeStruct((cols, width_x * width_y), BF16),
        ],
        in_specs=[smem()] * 4 + [vmem()] * 7,
        out_specs=[vmem()] * 2,
        scratch_shapes=[field] * 3 + [table] * 4 + [own_table] * 3,
        name="filter",
    )(flags, mat_diag, mat_cond, cheb_coef, flat, cell_ids, even, odd, strip, strip_even, strip_odd)
    return smooth.reshape(adjoint.shape), low


def ring_order(size):
    return [0] + list(range(1, size, 2)) + list(range(2, size, 2))[::-1]


def gathered_product(low, rows):
    size = lax.axis_size("cr")
    order = ring_order(size)
    me = lax.axis_index("cr")
    hop = [(order[i], order[(i + 1) % size]) for i in range(size)] if size > 1 else []
    before = [0] * size
    for a, b in hop:
        before[b] = a
    table = jnp.array(before, jnp.int32)
    products = []
    owners = []
    owner = me
    piece = low
    for step in range(size):
        following = lax.ppermute(piece, "cr", hop) if step < size - 1 else None
        products.append(
            lax.dot_general(piece, rows, (((1,), (1,)), ((), ())), preferred_element_type=F32)
        )
        owners.append(owner)
        piece = following
        owner = table[owner]
    return products, owners


def reduced(products, owners):
    size = len(products)
    cols, n_rows = products[0].shape
    size_x = lax.axis_size("sx")
    size_y = lax.axis_size("sy")
    plane = size_x * size_y
    share = size * cols // plane
    whole = jnp.zeros((size, cols, n_rows), F32)
    for product, owner in zip(products, owners):
        whole = lax.dynamic_update_slice(whole, product[None], (owner, 0, 0))
    whole = whole.reshape(size_x // 2, 2, size_y, share, n_rows)
    core = lax.axis_index("sx") % 2
    keep = lax.dynamic_index_in_dim(whole, core, 1, keepdims=False)
    send = lax.dynamic_index_in_dim(whole, 1 - core, 1, keepdims=False).astype(BF16)
    half = pairing(0, None, size_x, size_y)
    total = keep + lax.ppermute(send, ("sx", "sy"), half).astype(F32)
    total = total.reshape(plane // 2, share, n_rows)
    sy = lax.axis_index("sy")
    spot = (lax.axis_index("sx") // 2) * size_y + sy
    mine = lax.dynamic_index_in_dim(total, spot, 0, keepdims=False)
    arrived = []
    for shift in range(1, plane // 2):
        pairs = []
        for i in range(size_x):
            for j in range(size_y):
                other = ((i // 2) * size_y + j) ^ shift
                pairs.append((i * size_y + j, ((other // size_y) * 2 + i % 2) * size_y + other % size_y))
        out = lax.dynamic_index_in_dim(total, spot ^ shift, 0, keepdims=False).astype(BF16)
        arrived.append(lax.ppermute(out, ("sx", "sy"), pairs))
    for part in arrived:
        mine = mine + part.astype(F32)
    return mine.T


def on_device(adjoint, sensor_rows, cell_ids, mat_diag, mat_cond, cheb_coef):
    smoothed, low = filtered(adjoint, cell_ids, mat_diag, mat_cond, cheb_coef)
    rows = sensor_rows.reshape(sensor_rows.shape[0], -1)
    products, owners = gathered_product(low, rows)
    return smoothed, reduced(products, owners)


def solution(mesh):
    placed = (P("cr", "sx", "sy"), P("cr", "sx", "sy"), P("sx", "sy"), P(), P(), P())
    return jax.shard_map(
        on_device,
        mesh=mesh,
        in_specs=placed,
        out_specs=(P("cr", "sx", "sy"), P("cr", ("sx", "sy"))),
        check_vma=False,
    )
```

```python
import functools

import jax
import jax.numpy as jnp
from jax import lax
from jax.experimental import pallas as pl
from jax.experimental.pallas import tpu as pltpu
from jax.sharding import PartitionSpec as P

DEG = 8
SUB = 8
LANES = 128
SIDE = 2 * DEG
UNROLL = 4
CHUNKS = 2
VMEM_GRANT = 16 * 1024 * 1024
F32 = jnp.float32
BF16 = jnp.bfloat16


def partner(i, odd, size):
    j = i ^ 1 if not odd else ((i + 1) ^ 1) - 1
    return j if 0 <= j < size else None


def pairing(kind_x, kind_y, size_x, size_y):
    pairs = []
    for i in range(size_x):
        for j in range(size_y):
            a = i if kind_x is None else partner(i, kind_x, size_x)
            b = j if kind_y is None else partner(j, kind_y, size_y)
            if a is not None and b is not None:
                pairs.append((i * size_y + j, a * size_y + b))
    return pairs


def edge_lanes():
    place = lax.broadcasted_iota(jnp.int32, (SUB, LANES), 1) & (SIDE - 1)
    return jnp.where(place < DEG, DEG - 1 - place, LANES - 1 + DEG - place)


def lane_gather(tile, index):
    return jnp.take_along_axis(tile, index, axis=1, mode="promise_in_bounds")


def is_even(axis):
    return lax.axis_index(axis) % 2 == 0


def pack_kernel(groups, width_x, n_kinds, adj_ref, ids_ref, *out_refs):
    row_refs = out_refs[:2]
    strip_refs = out_refs[2:]
    upper_x = jnp.where(is_even("sx"), 1, 0)
    upper_y = jnp.where(is_even("sy"), 1, 0)
    index = edge_lanes()
    lane = lax.broadcasted_iota(jnp.int32, (SUB, LANES), 1)
    low_side = jnp.where((lane & (SIDE - 1)) < DEG, 1, 0)
    for which in range(2):
        upper = upper_x if which == 0 else 1 - upper_x
        base = pl.multiple_of(upper * (width_x - DEG), SUB)
        for row in range(DEG):
            for g in range(groups):
                row_refs[which][row * groups + g] = adj_ref[pl.ds(g * SUB * width_x + base + row, SUB, stride=width_x), :]
        row_refs[which][DEG * groups] = ids_ref[pl.ds(base, SUB), :].astype(F32) + 1.0
    for kind in range(n_kinds):
        upper = upper_y if kind == 0 else 1 - upper_y
        keep = (low_side ^ upper) == 1
        for row in range(width_x):
            strip = jnp.zeros((SUB, LANES), F32)
            for g in range(groups):
                tile = adj_ref[pl.ds(g * SUB * width_x + row, SUB, stride=width_x), :]
                strip = jnp.where((lane // SIDE) == g, lane_gather(tile, index), strip)
            strip_refs[3 * kind][row] = jnp.where(keep, strip, 0.0)
        for tile_x in range(width_x // SUB):
            ids = ids_ref[tile_x * SUB : (tile_x + 1) * SUB, :].astype(F32) + 1.0
            strip_refs[3 * kind][width_x + tile_x] = jnp.where(keep, lane_gather(ids, index), 0.0)
        for which in range(2):
            upper = upper_x if which == 0 else 1 - upper_x
            base = upper * (width_x - DEG)
            for row in range(DEG):
                strip_refs[3 * kind + 1 + which][row] = strip_refs[3 * kind][base + row]
            strip_refs[3 * kind + 1 + which][DEG] = strip_refs[3 * kind][width_x + upper * (width_x // SUB - 1)]


def power_terms():
    polys = [[1], [0, 1]]
    for _ in range(2, DEG + 1):
        doubled = [0] + [2 * t for t in polys[-1]]
        older = polys[-2] + [0] * (len(doubled) - len(polys[-2]))
        polys.append([p - q for p, q in zip(doubled, older)])
    return [[p[k] if k < len(p) else 0 for p in polys] for k in range(DEG + 1)]


def filter_kernel(
    groups, all_groups, offset, width_x, diag_ref, cond_ref, coef_ref, adj_ref, ids_ref, even_ref, odd_ref, strip_ref,
    strip_even_ref, strip_odd_ref, smooth_ref, low_ref, u_ref, a_ref, b_ref, cond_t, c2_t, d_t, cond_s, c2_s, d_s, inv_t,
):
    tall = width_x + 2 * DEG
    n_mat = diag_ref.shape[0]
    lane = lax.broadcasted_iota(jnp.int32, (SUB, LANES), 1)
    even_x = is_even("sx")
    power = []
    for terms in power_terms():
        parts = [coef_ref[j] if t == 1 else coef_ref[j] * float(t) for j, t in enumerate(terms) if t]
        power.append(functools.reduce(lambda p, q: p + q, parts))

    def lookup(ids, x0, cond_ref_t, c2_ref_t, d_ref_t):
        diag = jnp.zeros_like(ids)
        cond = jnp.zeros_like(ids)
        for m in range(n_mat):
            hit = ids == float(m + 1)
            diag = jnp.where(hit, diag_ref[m], diag)
            cond = jnp.where(hit, cond_ref[m], cond)
        cond_ref_t[x0 : x0 + SUB, :] = cond
        c2_ref_t[x0 : x0 + SUB, :] = cond * cond
        d_ref_t[x0 : x0 + SUB, :] = diag
        return cond

    def spread(ref, x):
        return ref[pl.ds(x, SUB, stride=0), :]

    repeat = lane & (SIDE - 1)
    for high in (False, True):
        x0 = tall - DEG if high else 0
        from_even = even_x if high else jnp.logical_not(even_x)
        ids = jnp.where(from_even, even_ref[DEG * all_groups], odd_ref[DEG * all_groups])
        lookup(ids, x0, cond_t, c2_t, d_t)
        ids = jnp.where(from_even, strip_even_ref[DEG], strip_odd_ref[DEG])
        lookup(lane_gather(ids, repeat), x0, cond_s, c2_s, d_s)
        for row in range(DEG):
            scale = spread(cond_t, x0 + row)
            for g in range(groups):
                at = row * all_groups + offset + g
                u_ref[x0 + row, g] = jnp.where(from_even, even_ref[at], odd_ref[at]) * scale
            tile = jnp.where(from_even, strip_even_ref[row], strip_odd_ref[row])
            u_ref[x0 + row, groups] = tile * spread(cond_s, x0 + row)
    for tile_x in range(width_x // SUB):
        x0 = DEG + tile_x * SUB
        cond = lookup(ids_ref[tile_x * SUB : (tile_x + 1) * SUB, :].astype(F32) + 1.0, x0, cond_t, c2_t, d_t)
        inv_t[tile_x * SUB : (tile_x + 1) * SUB, :] = 1.0 / cond
        lookup(lane_gather(strip_ref[width_x + tile_x], repeat), x0, cond_s, c2_s, d_s)
        for row in range(SUB):
            scale = spread(cond_t, x0 + row)
            for g in range(groups):
                start = (offset + g) * SUB * width_x + tile_x * SUB + row
                u_ref[x0 + row, g] = adj_ref[pl.ds(start, SUB, stride=width_x), :] * scale
            u_ref[x0 + row, groups] = strip_ref[tile_x * SUB + row] * spread(cond_s, x0 + row)

    first_lane = lane == 0
    last_lane = lane == LANES - 1
    place = lane & (SIDE - 1)
    at_high = place == DEG - 1
    at_low = place == DEG
    junction = lane // SIDE

    def across(tiles, strip, with_strip):
        sums = []
        meet = None
        for g, tile in enumerate(tiles):
            off = (offset + g) * SIDE + DEG
            edge = pltpu.roll(strip, LANES - off, 1)
            left = jnp.where(first_lane, edge, pltpu.roll(tile, 1, 1))
            right = jnp.where(last_lane, edge, pltpu.roll(tile, LANES - 1, 1))
            sums.append(left + right)
            if with_strip:
                moved = pltpu.roll(tile, off, 1)
                meet = moved if meet is None else jnp.where(junction == offset + g, moved, meet)
        if with_strip:
            up = jnp.where(at_high, meet, pltpu.roll(strip, LANES - 1, 1))
            down = jnp.where(at_low, meet, pltpu.roll(strip, 1, 1))
            sums.append(up + down)
        return sums

    def neighbours(src, x, count, with_strip):
        rows = [[src[x + r, g] for g in range(groups + 1)] for r in range(-1, count + 1)]
        out = []
        for r in range(1, count + 1):
            sums = across(rows[r][:groups], rows[r][groups], with_strip)
            sums = [s + (rows[r - 1][g] + rows[r + 1][g]) for g, s in enumerate(sums)]
            out.append((rows[r], sums))
        return out

    def swept(lo, body):
        n = tall - 2 * lo
        whole = n // UNROLL

        def run(i, carry):
            body(lo + i * UNROLL, UNROLL)
            return carry

        lax.fori_loop(0, whole, run, 0)
        if n % UNROLL:
            body(lo + whole * UNROLL, n % UNROLL)

    src = u_ref
    for order in range(DEG - 1, 0, -1):
        dst = a_ref if src is not a_ref else b_ref

        def body(x, count, order=order, src=src, dst=dst):
            for r, (tiles, sums) in enumerate(neighbours(src, x, count, True)):
                c2 = spread(c2_t, x + r)
                d = spread(d_t, x + r)
                c2s = spread(c2_s, x + r)
                ds = spread(d_s, x + r)
                for g in range(groups + 1):
                    cc, dd = (c2, d) if g < groups else (c2s, ds)
                    applied = dd * tiles[g] + cc * sums[g]
                    if order == DEG - 1:
                        value = power[order] * tiles[g] + power[DEG] * applied
                    else:
                        value = power[order] * u_ref[x + r, g] + applied
                    dst[x + r, g] = value

        swept(DEG - order, body)
        src = dst

    def last(x, count):
        for r, (tiles, sums) in enumerate(neighbours(src, x, count, False)):
            at = x + r - DEG
            cond = spread(cond_t, x + r)
            d = spread(d_t, x + r)
            inverse = spread(inv_t, at)
            out = []
            for g in range(groups):
                value = inverse * (power[0] * u_ref[x + r, g] + d * tiles[g]) + cond * sums[g]
                smooth_ref[pl.ds(g * SUB * width_x + at, SUB, stride=width_x), :] = value
                out.append(value)
            column = at * LANES if isinstance(at, int) else pl.multiple_of(at * LANES, LANES)
            for g in range(0, groups, 2):
                both = jnp.concatenate(out[g : g + 2], axis=0)
                low_ref[pl.ds(g * SUB, 2 * SUB), pl.ds(column, LANES)] = both.astype(BF16)

    swept(DEG, last)


def vmem():
    return pl.BlockSpec(memory_space=pltpu.VMEM)


def smem():
    return pl.BlockSpec(memory_space=pltpu.SMEM)


def filtered(adjoint, cell_ids, mat_diag, mat_cond, cheb_coef):
    cols, width_x, width_y = adjoint.shape
    groups = cols // SUB
    assert width_y == LANES and width_x % SUB == 0 and width_x >= DEG
    assert cols % SIDE == 0 and groups * SIDE <= LANES
    size_x = lax.axis_size("sx")
    size_y = lax.axis_size("sy")
    flat = adjoint.reshape(cols * width_x, width_y)
    n_kinds = 2 if size_y > 2 else 1
    row_shape = jax.ShapeDtypeStruct((DEG * groups + 1, SUB, LANES), F32)
    strip_shape = jax.ShapeDtypeStruct((width_x + width_x // SUB, SUB, LANES), F32)
    corner_shape = jax.ShapeDtypeStruct((DEG + 1, SUB, LANES), F32)
    packed = pl.pallas_call(
        functools.partial(pack_kernel, groups, width_x, n_kinds),
        out_shape=[row_shape] * 2 + [strip_shape, corner_shape, corner_shape] * n_kinds,
        in_specs=[vmem(), vmem()],
        out_specs=[vmem()] * (2 + 3 * n_kinds),
        compiler_params=pltpu.CompilerParams(vmem_limit_bytes=VMEM_GRANT),
        name="pack",
    )(flat, cell_ids)

    def swap(value, kind_x, kind_y):
        pairs = pairing(kind_x, kind_y, size_x, size_y)
        if not pairs:
            return jnp.zeros_like(value)
        return lax.ppermute(value, ("sx", "sy"), pairs)

    odd = swap(packed[1], 1, None)
    even = swap(packed[0], 0, None)
    strips = []
    for kind in range(n_kinds):
        strips.append(
            (
                swap(packed[2 + 3 * kind], None, kind),
                swap(packed[3 + 3 * kind], 0, kind),
                swap(packed[4 + 3 * kind], 1, kind),
            )
        )
    strip, strip_even, strip_odd = (functools.reduce(jnp.add, part) for part in zip(*strips))
    tall = width_x + 2 * DEG
    n_chunks = CHUNKS if groups % (2 * CHUNKS) == 0 else 1
    part = groups // n_chunks
    table = pltpu.VMEM((tall, LANES), F32)
    field = pltpu.VMEM((tall, part + 1, SUB, LANES), F32)
    smooth = []
    low = []
    for chunk in range(n_chunks):
        one, other = pl.pallas_call(
            functools.partial(filter_kernel, part, groups, chunk * part, width_x),
            out_shape=[
                jax.ShapeDtypeStruct((part * SUB * width_x, width_y), F32),
                jax.ShapeDtypeStruct((part * SUB, width_x * width_y), BF16),
            ],
            in_specs=[smem()] * 3 + [vmem()] * 7,
            out_specs=[vmem()] * 2,
            scratch_shapes=[field] * 3 + [table] * 6 + [pltpu.VMEM((width_x, LANES), F32)],
            compiler_params=pltpu.CompilerParams(vmem_limit_bytes=VMEM_GRANT),
            cost_estimate=pl.CostEstimate(flops=part * 3000000, bytes_accessed=part * 200000, transcendentals=0),
            name=f"filter{chunk}",
        )(mat_diag, mat_cond, cheb_coef, flat, cell_ids, even, odd, strip, strip_even, strip_odd)
        smooth.append(one)
        low.append(other)
    smooth = smooth[0] if n_chunks == 1 else jnp.concatenate(smooth)
    return smooth.reshape(adjoint.shape), low


def ring_order(size):
    return [0] + list(range(1, size, 2)) + list(range(2, size, 2))[::-1]


def stepped(before, me, steps):
    found = jnp.int32(0)
    for start in range(len(before)):
        spot = start
        for _ in range(steps):
            spot = before[spot]
        found = jnp.where(me == start, spot, found)
    return found


def gathered_product(low, rows):
    size = lax.axis_size("cr")
    order = ring_order(size)
    me = lax.axis_index("cr")
    hop = [(order[i], order[(i + 1) % size]) for i in range(size)] if size > 1 else []
    before = [0] * size
    for a, b in hop:
        before[b] = a
    products = []
    owners = []
    pieces = list(low)
    for step in range(size):
        following = [lax.ppermute(p, "cr", hop) for p in pieces] if step < size - 1 else None
        piece = pieces[0] if len(pieces) == 1 else jnp.concatenate(pieces)
        products.append(lax.dot_general(piece, rows, (((1,), (1,)), ((), ())), preferred_element_type=F32))
        owners.append(stepped(before, me, step))
        pieces = following
    return products, owners


def reduced(products, owners):
    size = len(products)
    cols, n_rows = products[0].shape
    size_x = lax.axis_size("sx")
    size_y = lax.axis_size("sy")
    plane = size_x * size_y
    share = size * cols // plane
    whole = jnp.zeros((size, cols, n_rows), F32)
    for product, owner in zip(products, owners):
        whole = lax.dynamic_update_slice(whole, product[None], (owner, 0, 0))
    whole = whole.reshape(size_x // 2, 2, size_y, share, n_rows)
    core = lax.axis_index("sx") % 2
    keep = lax.dynamic_index_in_dim(whole, core, 1, keepdims=False)
    send = lax.dynamic_index_in_dim(whole, 1 - core, 1, keepdims=False).astype(BF16)
    half = pairing(0, None, size_x, size_y)
    total = keep + lax.ppermute(send, ("sx", "sy"), half).astype(F32)
    total = total.reshape(plane // 2, share, n_rows)
    sy = lax.axis_index("sy")
    spot = (lax.axis_index("sx") // 2) * size_y + sy
    mine = lax.dynamic_index_in_dim(total, spot, 0, keepdims=False)
    arrived = []
    for shift in range(1, plane // 2):
        pairs = []
        for i in range(size_x):
            for j in range(size_y):
                other = ((i // 2) * size_y + j) ^ shift
                pairs.append((i * size_y + j, ((other // size_y) * 2 + i % 2) * size_y + other % size_y))
        out = lax.dynamic_index_in_dim(total, spot ^ shift, 0, keepdims=False).astype(BF16)
        arrived.append(lax.ppermute(out, ("sx", "sy"), pairs))
    for part in arrived:
        mine = mine + part.astype(F32)
    return mine.T


def on_device(adjoint, sensor_rows, cell_ids, mat_diag, mat_cond, cheb_coef):
    smoothed, low = filtered(adjoint, cell_ids, mat_diag, mat_cond, cheb_coef)
    rows = sensor_rows.reshape(sensor_rows.shape[0], -1)
    products, owners = gathered_product(low, rows)
    return smoothed, reduced(products, owners)


def solution(mesh):
    placed = (P("cr", "sx", "sy"), P("cr", "sx", "sy"), P("sx", "sy"), P(), P(), P())
    return jax.shard_map(
        on_device,
        mesh=mesh,
        in_specs=placed,
        out_specs=(P("cr", "sx", "sy"), P("cr", ("sx", "sy"))),
        check_vma=False,
    )
```

```python
import functools

import jax
import jax.numpy as jnp
from jax import lax
from jax.experimental import pallas as pl
from jax.experimental.pallas import tpu as pltpu
from jax.sharding import PartitionSpec as P

DEG = 8
SUB = 8
LANES = 128
SIDE = 2 * DEG
UNROLL = 8
CHUNKS = 2
VMEM_GRANT = 16 * 1024 * 1024
F32 = jnp.float32
BF16 = jnp.bfloat16


def partner(i, odd, size):
    j = i ^ 1 if not odd else ((i + 1) ^ 1) - 1
    return j if 0 <= j < size else None


def pairing(kind_x, kind_y, size_x, size_y):
    pairs = []
    for i in range(size_x):
        for j in range(size_y):
            a = i if kind_x is None else partner(i, kind_x, size_x)
            b = j if kind_y is None else partner(j, kind_y, size_y)
            if a is not None and b is not None:
                pairs.append((i * size_y + j, a * size_y + b))
    return pairs


def edge_lanes():
    place = lax.broadcasted_iota(jnp.int32, (SUB, LANES), 1) & (SIDE - 1)
    return jnp.where(place < DEG, DEG - 1 - place, LANES - 1 + DEG - place)


def lane_gather(tile, index):
    return jnp.take_along_axis(tile, index, axis=1, mode="promise_in_bounds")


def is_even(axis):
    return lax.axis_index(axis) % 2 == 0


def pack_kernel(groups, width_x, n_kinds, *refs):
    adj_hbm, ids_hbm, diag_hbm, cond_hbm, coef_hbm, adj_ref, ids_ref, params_ref = refs[:8]
    diag_ref, cond_ref, coef_ref, sem = refs[-4:]
    row_refs = refs[8:10]
    strip_refs = refs[10:-4]
    pairs = ((adj_hbm, adj_ref), (ids_hbm, ids_ref), (diag_hbm, diag_ref), (cond_hbm, cond_ref), (coef_hbm, coef_ref))
    copies = [pltpu.make_async_copy(src, dst, sem.at[i]) for i, (src, dst) in enumerate(pairs)]
    for copy in copies:
        copy.start()
    for copy in copies:
        copy.wait()
    upper_x = jnp.where(is_even("sx"), 1, 0)
    upper_y = jnp.where(is_even("sy"), 1, 0)
    index = edge_lanes()
    lane = lax.broadcasted_iota(jnp.int32, (SUB, LANES), 1)
    low_side = jnp.where((lane & (SIDE - 1)) < DEG, 1, 0)
    for which in range(2):
        upper = upper_x if which == 0 else 1 - upper_x
        base = pl.multiple_of(upper * (width_x - DEG), SUB)
        for row in range(DEG):
            for g in range(groups):
                row_refs[which][row * groups + g] = adj_ref[pl.ds(g * SUB * width_x + base + row, SUB, stride=width_x), :]
        row_refs[which][DEG * groups] = ids_ref[pl.ds(base, SUB), :].astype(F32) + 1.0
    for kind in range(n_kinds):
        upper = upper_y if kind == 0 else 1 - upper_y
        keep = (low_side ^ upper) == 1
        for row in range(width_x):
            strip = jnp.zeros((SUB, LANES), F32)
            for g in range(groups):
                tile = adj_ref[pl.ds(g * SUB * width_x + row, SUB, stride=width_x), :]
                strip = jnp.where((lane // SIDE) == g, lane_gather(tile, index), strip)
            strip_refs[3 * kind][row] = jnp.where(keep, strip, 0.0)
        for tile_x in range(width_x // SUB):
            ids = ids_ref[tile_x * SUB : (tile_x + 1) * SUB, :].astype(F32) + 1.0
            strip_refs[3 * kind][width_x + tile_x] = jnp.where(keep, lane_gather(ids, index), 0.0)
        for which in range(2):
            upper = upper_x if which == 0 else 1 - upper_x
            base = upper * (width_x - DEG)
            for row in range(DEG):
                strip_refs[3 * kind + 1 + which][row] = strip_refs[3 * kind][base + row]
            strip_refs[3 * kind + 1 + which][DEG] = strip_refs[3 * kind][width_x + upper * (width_x // SUB - 1)]
    for i, ref in enumerate((diag_ref, cond_ref)):
        tile = jnp.zeros((SUB, LANES), F32)
        for m in range(ref.shape[0]):
            tile = jnp.where(lane == m + 1, ref[m], tile)
        params_ref[i] = tile
    tile = jnp.zeros((SUB, LANES), F32)
    for k, terms in enumerate(power_terms()):
        parts = [coef_ref[j] * float(t) for j, t in enumerate(terms) if t]
        tile = jnp.where(lane == k, functools.reduce(lambda p, q: p + q, parts), tile)
    params_ref[2] = tile


def power_terms():
    polys = [[1], [0, 1]]
    for _ in range(2, DEG + 1):
        doubled = [0] + [2 * t for t in polys[-1]]
        older = polys[-2] + [0] * (len(doubled) - len(polys[-2]))
        polys.append([p - q for p, q in zip(doubled, older)])
    return [[p[k] if k < len(p) else 0 for p in polys] for k in range(DEG + 1)]


COND, COND2, DIAG, COND_S, COND2_S, DIAG_S, INVERSE = range(7)


def filter_kernel(groups, all_groups, offset, width_x, first, *refs):
    params_ref, adj_ref, ids_ref, even_ref, odd_ref, strip_ref, strip_even_ref, strip_odd_ref = refs[:8]
    if first:
        smooth_ref, low_ref, table = refs[8:11]
    else:
        table, smooth_ref, low_ref = refs[8:11]
    u_ref, a_ref, b_ref, y_ref, power = refs[11:]
    tall = width_x + 2 * DEG
    lane = lax.broadcasted_iota(jnp.int32, (SUB, LANES), 1)
    even_x = is_even("sx")
    for k in range(DEG + 1):
        power[k] = lane_gather(params_ref[2], jnp.full((SUB, LANES), k, jnp.int32))

    def lookup(ids, x0, strip):
        ids = ids.astype(jnp.int32)
        cond = lane_gather(params_ref[1], ids)
        table[COND_S if strip else COND, x0 : x0 + SUB, :] = cond
        table[COND2_S if strip else COND2, x0 : x0 + SUB, :] = cond * cond
        table[DIAG_S if strip else DIAG, x0 : x0 + SUB, :] = lane_gather(params_ref[0], ids)
        return cond

    def spread(which, x):
        return table[which, pl.ds(x, SUB, stride=0), :]

    first_lane = lane == 0
    last_lane = lane == LANES - 1
    place = lane & (SIDE - 1)
    at_high = place == DEG - 1
    at_low = place == DEG
    junction = lane // SIDE

    def across(tiles):
        sums = []
        meet = None
        strip = tiles[groups]
        for g, tile in enumerate(tiles[:groups]):
            off = (offset + g) * SIDE + DEG
            edge = pltpu.roll(strip, LANES - off, 1)
            left = jnp.where(first_lane, edge, pltpu.roll(tile, 1, 1))
            right = jnp.where(last_lane, edge, pltpu.roll(tile, LANES - 1, 1))
            sums.append(left + right)
            moved = pltpu.roll(tile, off, 1)
            meet = moved if meet is None else jnp.where(junction == offset + g, moved, meet)
        up = jnp.where(at_high, meet, pltpu.roll(strip, LANES - 1, 1))
        down = jnp.where(at_low, meet, pltpu.roll(strip, 1, 1))
        sums.append(up + down)
        return sums

    def place_row(x, tiles):
        for g in range(groups + 1):
            u_ref[x, g] = tiles[g]
        for g, total in enumerate(across(tiles)):
            y_ref[x, g] = total

    repeat = lane & (SIDE - 1)
    if first:
        for high in (False, True):
            x0 = tall - DEG if high else 0
            from_even = even_x if high else jnp.logical_not(even_x)
            lookup(jnp.where(from_even, even_ref[DEG * all_groups], odd_ref[DEG * all_groups]), x0, False)
            ids = jnp.where(from_even, strip_even_ref[DEG], strip_odd_ref[DEG])
            lookup(lane_gather(ids, repeat), x0, True)
        for tile_x in range(width_x // SUB):
            x0 = DEG + tile_x * SUB
            cond = lookup(ids_ref[tile_x * SUB : (tile_x + 1) * SUB, :] + 1, x0, False)
            table[INVERSE, x0 : x0 + SUB, :] = 1.0 / cond
            lookup(lane_gather(strip_ref[width_x + tile_x], repeat), x0, True)
    for high in (False, True):
        x0 = tall - DEG if high else 0
        from_even = even_x if high else jnp.logical_not(even_x)
        for row in range(DEG):
            scale = spread(COND, x0 + row)
            tiles = []
            for g in range(groups):
                at = row * all_groups + offset + g
                tiles.append(jnp.where(from_even, even_ref[at], odd_ref[at]) * scale)
            strip = jnp.where(from_even, strip_even_ref[row], strip_odd_ref[row])
            place_row(x0 + row, tiles + [strip * spread(COND_S, x0 + row)])
    for row in range(width_x):
        x = DEG + row
        scale = spread(COND, x)
        tiles = []
        for g in range(groups):
            tiles.append(adj_ref[pl.ds((offset + g) * SUB * width_x + row, SUB, stride=width_x), :] * scale)
        place_row(x, tiles + [strip_ref[row] * spread(COND_S, x)])

    def swept(lo, body, after=None):
        n = tall - 2 * lo
        blocks = n // UNROLL
        rest = n % UNROLL

        def step(x, count, x_before, count_before):
            body(x, count, None if after is None or not count_before else lambda: after(x_before, count_before))

        step(lo, UNROLL, None, 0)

        def run(i, carry):
            step(lo + i * UNROLL, UNROLL, lo + (i - 1) * UNROLL, UNROLL)
            return carry

        lax.fori_loop(1, blocks, run, 0)
        x = lo + blocks * UNROLL
        if rest:
            step(x, rest, x - UNROLL, UNROLL)
            if after is not None:
                for store in after(x, rest):
                    store()
        elif after is not None:
            for store in after(x - UNROLL, UNROLL):
                store()

    src = u_ref
    for order in range(DEG - 1, 0, -1):
        dst = a_ref if src is not a_ref else b_ref

        def body(x, count, before, order=order, src=src, dst=dst):
            rows = [[src[x + r, g] for g in range(groups + 1)] for r in range(-1, count + 1)]
            sums = [[y_ref[x + r, g] for g in range(groups + 1)] for r in range(count)]
            starts = rows[1:-1] if order == DEG - 1 else [[u_ref[x + r, g] for g in range(groups + 1)] for r in range(count)]
            pending = before() if before is not None else []
            coef = power[order]
            for r in range(count):
                c2, d, c2s, ds = (spread(which, x + r) for which in (COND2, DIAG, COND2_S, DIAG_S))
                for g in range(groups + 1):
                    cc, dd = (c2, d) if g < groups else (c2s, ds)
                    total = sums[r][g] + (rows[r][g] + rows[r + 2][g])
                    applied = dd * rows[r + 1][g] + cc * total
                    if order == DEG - 1:
                        applied = power[DEG] * applied
                    dst[x + r, g] = coef * starts[r][g] + applied
            for store in pending:
                store()

        def after(x, count, dst=dst):
            rows = [[dst[x + r, g] for g in range(groups + 1)] for r in range(count)]
            stores = []
            for r in range(count):
                for g, total in enumerate(across(rows[r])):
                    def put(r=r, g=g, total=total):
                        y_ref[x + r, g] = total
                    stores.append(put)
            return stores

        swept(DEG - order, body, after)
        src = dst

    def last(x, count, before):
        rows = [[src[x + r, g] for g in range(groups)] for r in range(-1, count + 1)]
        for r in range(count):
            at = x + r - DEG
            cond, d, inverse = (spread(which, x + r) for which in (COND, DIAG, INVERSE))
            out = []
            for g in range(groups):
                total = y_ref[x + r, g] + (rows[r][g] + rows[r + 2][g])
                value = inverse * (power[0] * u_ref[x + r, g] + d * rows[r + 1][g]) + cond * total
                smooth_ref[pl.ds(g * SUB * width_x + at, SUB, stride=width_x), :] = value
                out.append(value)
            column = at * LANES if isinstance(at, int) else pl.multiple_of(at * LANES, LANES)
            for g in range(0, groups, 2):
                both = jnp.concatenate(out[g : g + 2], axis=0)
                low_ref[pl.ds(g * SUB, 2 * SUB), pl.ds(column, LANES)] = both.astype(BF16)

    swept(DEG, last)


def vmem():
    return pl.BlockSpec(memory_space=pltpu.VMEM)


def hbm():
    return pl.BlockSpec(memory_space=pltpu.HBM)


def filtered(adjoint, cell_ids, mat_diag, mat_cond, cheb_coef):
    cols, width_x, width_y = adjoint.shape
    groups = cols // SUB
    assert width_y == LANES and width_x % SUB == 0 and width_x >= DEG
    assert cols % SIDE == 0 and groups * SIDE <= LANES
    size_x = lax.axis_size("sx")
    size_y = lax.axis_size("sy")
    flat = adjoint.reshape(cols * width_x, width_y)
    n_kinds = 2 if size_y > 2 else 1
    row_shape = jax.ShapeDtypeStruct((DEG * groups + 1, SUB, LANES), F32)
    strip_shape = jax.ShapeDtypeStruct((width_x + width_x // SUB, SUB, LANES), F32)
    corner_shape = jax.ShapeDtypeStruct((DEG + 1, SUB, LANES), F32)
    small = [pltpu.SMEM(v.shape, F32) for v in (mat_diag, mat_cond, cheb_coef)]
    flat, ids, params, *packed = pl.pallas_call(
        functools.partial(pack_kernel, groups, width_x, n_kinds),
        out_shape=[
            jax.ShapeDtypeStruct(flat.shape, F32),
            jax.ShapeDtypeStruct(cell_ids.shape, jnp.int32),
            jax.ShapeDtypeStruct((3, SUB, LANES), F32),
        ]
        + [row_shape] * 2
        + [strip_shape, corner_shape, corner_shape] * n_kinds,
        in_specs=[hbm()] * 5,
        out_specs=[vmem()] * (5 + 3 * n_kinds),
        scratch_shapes=small + [pltpu.SemaphoreType.DMA((5,))],
        compiler_params=pltpu.CompilerParams(vmem_limit_bytes=VMEM_GRANT),
        name="pack",
    )(flat, cell_ids, mat_diag, mat_cond, cheb_coef)

    def swap(value, kind_x, kind_y):
        pairs = pairing(kind_x, kind_y, size_x, size_y)
        if not pairs:
            return jnp.zeros_like(value)
        return lax.ppermute(value, ("sx", "sy"), pairs)

    odd = swap(packed[1], 1, None)
    even = swap(packed[0], 0, None)
    strips = []
    for kind in range(n_kinds):
        strips.append(
            (
                swap(packed[2 + 3 * kind], None, kind),
                swap(packed[3 + 3 * kind], 0, kind),
                swap(packed[4 + 3 * kind], 1, kind),
            )
        )
    strip, strip_even, strip_odd = (functools.reduce(jnp.add, part) for part in zip(*strips))
    tall = width_x + 2 * DEG
    n_chunks = CHUNKS if groups % (2 * CHUNKS) == 0 else 1
    part = groups // n_chunks
    table_shape = jax.ShapeDtypeStruct((7, tall, LANES), F32)
    field = pltpu.VMEM((tall, part + 1, SUB, LANES), F32)
    smooth = []
    low = []
    table = []
    for chunk in range(n_chunks):
        out_shape = [
            jax.ShapeDtypeStruct((part * SUB * width_x, width_y), F32),
            jax.ShapeDtypeStruct((part * SUB, width_x * width_y), BF16),
        ]
        got = pl.pallas_call(
            functools.partial(filter_kernel, part, groups, chunk * part, width_x, chunk == 0),
            out_shape=out_shape + ([table_shape] if chunk == 0 else []),
            in_specs=[vmem()] * (8 + len(table)),
            out_specs=[vmem()] * (3 if chunk == 0 else 2),
            scratch_shapes=[field] * 4 + [pltpu.VMEM((DEG + 1, SUB, LANES), F32)],
            compiler_params=pltpu.CompilerParams(vmem_limit_bytes=VMEM_GRANT),
            cost_estimate=pl.CostEstimate(flops=part * 3000000, bytes_accessed=part * 200000, transcendentals=0),
            name=f"filter{chunk}",
        )(params, flat, ids, even, odd, strip, strip_even, strip_odd, *table)
        smooth.append(got[0])
        low.append(got[1])
        if chunk == 0:
            table = got[2:]
    smooth = smooth[0] if n_chunks == 1 else jnp.concatenate(smooth)
    return smooth.reshape(adjoint.shape), low


def ring_order(size):
    return [0] + list(range(1, size, 2)) + list(range(2, size, 2))[::-1]


def stepped(before, me, steps):
    found = jnp.int32(0)
    for start in range(len(before)):
        spot = start
        for _ in range(steps):
            spot = before[spot]
        found = jnp.where(me == start, spot, found)
    return found


def gathered_product(low, rows):
    size = lax.axis_size("cr")
    order = ring_order(size)
    me = lax.axis_index("cr")
    hop = [(order[i], order[(i + 1) % size]) for i in range(size)] if size > 1 else []
    before = [0] * size
    for a, b in hop:
        before[b] = a
    products = []
    owners = []
    pieces = list(low)
    for step in range(size):
        following = [lax.ppermute(p, "cr", hop) for p in pieces] if step < size - 1 else None
        piece = pieces[0] if len(pieces) == 1 else jnp.concatenate(pieces)
        products.append(lax.dot_general(piece, rows, (((1,), (1,)), ((), ())), preferred_element_type=F32))
        owners.append(stepped(before, me, step))
        pieces = following
    return products, owners


def reduced(products, owners):
    size = len(products)
    cols, n_rows = products[0].shape
    size_x = lax.axis_size("sx")
    size_y = lax.axis_size("sy")
    plane = size_x * size_y
    share = size * cols // plane
    whole = jnp.zeros((size, cols, n_rows), F32)
    for product, owner in zip(products, owners):
        whole = lax.dynamic_update_slice(whole, product[None], (owner, 0, 0))
    whole = whole.reshape(size_x // 2, 2, size_y, share, n_rows)
    core = lax.axis_index("sx") % 2
    keep = lax.dynamic_index_in_dim(whole, core, 1, keepdims=False)
    send = lax.dynamic_index_in_dim(whole, 1 - core, 1, keepdims=False).astype(BF16)
    half = pairing(0, None, size_x, size_y)
    total = keep + lax.ppermute(send, ("sx", "sy"), half).astype(F32)
    total = total.reshape(plane // 2, share, n_rows)
    sy = lax.axis_index("sy")
    spot = (lax.axis_index("sx") // 2) * size_y + sy
    mine = lax.dynamic_index_in_dim(total, spot, 0, keepdims=False)
    arrived = []
    for shift in range(1, plane // 2):
        pairs = []
        for i in range(size_x):
            for j in range(size_y):
                other = ((i // 2) * size_y + j) ^ shift
                pairs.append((i * size_y + j, ((other // size_y) * 2 + i % 2) * size_y + other % size_y))
        out = lax.dynamic_index_in_dim(total, spot ^ shift, 0, keepdims=False).astype(BF16)
        arrived.append(lax.ppermute(out, ("sx", "sy"), pairs))
    for part in arrived:
        mine = mine + part.astype(F32)
    return mine.T


def on_device(adjoint, sensor_rows, cell_ids, mat_diag, mat_cond, cheb_coef):
    smoothed, low = filtered(adjoint, cell_ids, mat_diag, mat_cond, cheb_coef)
    rows = sensor_rows.reshape(sensor_rows.shape[0], -1)
    products, owners = gathered_product(low, rows)
    return smoothed, reduced(products, owners)


def solution(mesh):
    placed = (P("cr", "sx", "sy"), P("cr", "sx", "sy"), P("sx", "sy"), P(), P(), P())
    return jax.shard_map(
        on_device,
        mesh=mesh,
        in_specs=placed,
        out_specs=(P("cr", "sx", "sy"), P("cr", ("sx", "sy"))),
        check_vma=False,
    )
```

```python
import functools

import jax
import jax.numpy as jnp
from jax import lax
from jax.experimental import pallas as pl
from jax.experimental.pallas import tpu as pltpu
from jax.sharding import PartitionSpec as P


DEG = 8
SUB = 8
LANES = 128
SIDE = 2 * DEG
UNROLL = 8
CHUNKS = 2
VMEM_GRANT = 16 * 1024 * 1024
F32 = jnp.float32
BF16 = jnp.bfloat16


def partner(i, odd, size):
    j = i ^ 1 if not odd else ((i + 1) ^ 1) - 1
    return j if 0 <= j < size else None


def pairing(kind_x, kind_y, size_x, size_y):
    pairs = []
    for i in range(size_x):
        for j in range(size_y):
            a = i if kind_x is None else partner(i, kind_x, size_x)
            b = j if kind_y is None else partner(j, kind_y, size_y)
            if a is not None and b is not None:
                pairs.append((i * size_y + j, a * size_y + b))
    return pairs


def edge_lanes():
    place = lax.broadcasted_iota(jnp.int32, (SUB, LANES), 1) & (SIDE - 1)
    return jnp.where(place < DEG, DEG - 1 - place, LANES - 1 + DEG - place)


def lane_gather(tile, index):
    return jnp.take_along_axis(tile, index, axis=1, mode="promise_in_bounds")


def is_even(axis):
    return lax.axis_index(axis) % 2 == 0


def pack_kernel(groups, width_x, n_kinds, *refs):
    adj_hbm, ids_hbm, diag_hbm, cond_hbm, coef_hbm, adj_ref, ids_ref, params_ref = refs[:8]
    diag_ref, cond_ref, coef_ref, sem = refs[-4:]
    row_refs = refs[8:10]
    strip_refs = refs[10:-4]
    pairs = ((adj_hbm, adj_ref), (ids_hbm, ids_ref), (diag_hbm, diag_ref), (cond_hbm, cond_ref), (coef_hbm, coef_ref))
    copies = [pltpu.make_async_copy(src, dst, sem.at[i]) for i, (src, dst) in enumerate(pairs)]
    for copy in copies:
        copy.start()
    for copy in copies:
        copy.wait()
    upper_x = jnp.where(is_even("sx"), 1, 0)
    upper_y = jnp.where(is_even("sy"), 1, 0)
    index = edge_lanes()
    lane = lax.broadcasted_iota(jnp.int32, (SUB, LANES), 1)
    low_side = jnp.where((lane & (SIDE - 1)) < DEG, 1, 0)
    for which in range(2):
        upper = upper_x if which == 0 else 1 - upper_x
        base = pl.multiple_of(upper * (width_x - DEG), SUB)
        for row in range(DEG):
            for g in range(groups):
                row_refs[which][row * groups + g] = adj_ref[pl.ds(g * SUB * width_x + base + row, SUB, stride=width_x), :]
        row_refs[which][DEG * groups] = ids_ref[pl.ds(base, SUB), :].astype(F32) + 1.0
    for kind in range(n_kinds):
        upper = upper_y if kind == 0 else 1 - upper_y
        keep = (low_side ^ upper) == 1
        for row in range(width_x):
            strip = jnp.zeros((SUB, LANES), F32)
            for g in range(groups):
                tile = adj_ref[pl.ds(g * SUB * width_x + row, SUB, stride=width_x), :]
                strip = jnp.where((lane // SIDE) == g, lane_gather(tile, index), strip)
            strip_refs[3 * kind][row] = jnp.where(keep, strip, 0.0)
        for tile_x in range(width_x // SUB):
            ids = ids_ref[tile_x * SUB : (tile_x + 1) * SUB, :].astype(F32) + 1.0
            strip_refs[3 * kind][width_x + tile_x] = jnp.where(keep, lane_gather(ids, index), 0.0)
        for which in range(2):
            upper = upper_x if which == 0 else 1 - upper_x
            base = upper * (width_x - DEG)
            for row in range(DEG):
                strip_refs[3 * kind + 1 + which][row] = strip_refs[3 * kind][base + row]
            strip_refs[3 * kind + 1 + which][DEG] = strip_refs[3 * kind][width_x + upper * (width_x // SUB - 1)]
    for i, ref in enumerate((diag_ref, cond_ref)):
        tile = jnp.zeros((SUB, LANES), F32)
        for m in range(ref.shape[0]):
            tile = jnp.where(lane == m + 1, ref[m], tile)
        params_ref[i] = tile
    tile = jnp.zeros((SUB, LANES), F32)
    for k, terms in enumerate(power_terms()):
        parts = [coef_ref[j] * float(t) for j, t in enumerate(terms) if t]
        tile = jnp.where(lane == k, functools.reduce(lambda p, q: p + q, parts), tile)
    params_ref[2] = tile


def power_terms():
    polys = [[1], [0, 1]]
    for _ in range(2, DEG + 1):
        doubled = [0] + [2 * t for t in polys[-1]]
        older = polys[-2] + [0] * (len(doubled) - len(polys[-2]))
        polys.append([p - q for p, q in zip(doubled, older)])
    return [[p[k] if k < len(p) else 0 for p in polys] for k in range(DEG + 1)]


COND, COND2, DIAG, COND_S, COND2_S, DIAG_S, INVERSE = range(7)


def filter_kernel(groups, all_groups, offset, width_x, first, *refs):
    params_ref, adj_ref, ids_ref, even_ref, odd_ref, strip_ref, strip_even_ref, strip_odd_ref = refs[:8]
    if first:
        smooth_ref, low_ref, table = refs[8:11]
    else:
        table, smooth_ref, low_ref = refs[8:11]
    u_ref, a_ref, b_ref, y_ref, power = refs[11:]
    tall = width_x + 2 * DEG
    lane = lax.broadcasted_iota(jnp.int32, (SUB, LANES), 1)
    even_x = is_even("sx")
    for k in range(DEG + 1):
        power[k] = lane_gather(params_ref[2], jnp.full((SUB, LANES), k, jnp.int32))

    def lookup(ids, x0, strip):
        ids = ids.astype(jnp.int32)
        cond = lane_gather(params_ref[1], ids)
        table[COND_S if strip else COND, x0 : x0 + SUB, :] = cond
        table[COND2_S if strip else COND2, x0 : x0 + SUB, :] = cond * cond
        table[DIAG_S if strip else DIAG, x0 : x0 + SUB, :] = lane_gather(params_ref[0], ids)
        return cond

    def spread(which, x):
        return table[which, pl.ds(x, SUB, stride=0), :]

    first_lane = lane == 0
    last_lane = lane == LANES - 1
    place = lane & (SIDE - 1)
    at_high = place == DEG - 1
    at_low = place == DEG
    junction = lane // SIDE

    def across(tiles):
        sums = []
        meet = None
        strip = tiles[groups]
        for g, tile in enumerate(tiles[:groups]):
            off = (offset + g) * SIDE + DEG
            edge = pltpu.roll(strip, LANES - off, 1)
            left = jnp.where(first_lane, edge, pltpu.roll(tile, 1, 1))
            right = jnp.where(last_lane, edge, pltpu.roll(tile, LANES - 1, 1))
            sums.append(left + right)
            moved = pltpu.roll(tile, off, 1)
            meet = moved if meet is None else jnp.where(junction == offset + g, moved, meet)
        up = jnp.where(at_high, meet, pltpu.roll(strip, LANES - 1, 1))
        down = jnp.where(at_low, meet, pltpu.roll(strip, 1, 1))
        sums.append(up + down)
        return sums

    def place_row(x, tiles):
        for g in range(groups + 1):
            u_ref[x, g] = tiles[g]
        for g, total in enumerate(across(tiles)):
            y_ref[x, g] = total

    repeat = lane & (SIDE - 1)
    if first:
        for high in (False, True):
            x0 = tall - DEG if high else 0
            from_even = even_x if high else jnp.logical_not(even_x)
            lookup(jnp.where(from_even, even_ref[DEG * all_groups], odd_ref[DEG * all_groups]), x0, False)
            ids = jnp.where(from_even, strip_even_ref[DEG], strip_odd_ref[DEG])
            lookup(lane_gather(ids, repeat), x0, True)
        for tile_x in range(width_x // SUB):
            x0 = DEG + tile_x * SUB
            cond = lookup(ids_ref[tile_x * SUB : (tile_x + 1) * SUB, :] + 1, x0, False)
            table[INVERSE, x0 : x0 + SUB, :] = 1.0 / cond
            lookup(lane_gather(strip_ref[width_x + tile_x], repeat), x0, True)
    for high in (False, True):
        x0 = tall - DEG if high else 0
        from_even = even_x if high else jnp.logical_not(even_x)
        for row in range(DEG):
            scale = spread(COND, x0 + row)
            tiles = []
            for g in range(groups):
                at = row * all_groups + offset + g
                tiles.append(jnp.where(from_even, even_ref[at], odd_ref[at]) * scale)
            strip = jnp.where(from_even, strip_even_ref[row], strip_odd_ref[row])
            place_row(x0 + row, tiles + [strip * spread(COND_S, x0 + row)])
    for row in range(width_x):
        x = DEG + row
        scale = spread(COND, x)
        tiles = []
        for g in range(groups):
            tiles.append(adj_ref[pl.ds((offset + g) * SUB * width_x + row, SUB, stride=width_x), :] * scale)
        place_row(x, tiles + [strip_ref[row] * spread(COND_S, x)])

    def swept(lo, body, after=None):
        n = tall - 2 * lo
        blocks = n // UNROLL
        rest = n % UNROLL

        def step(x, count, x_before, count_before):
            body(x, count, None if after is None or not count_before else lambda: after(x_before, count_before))

        step(lo, UNROLL, None, 0)

        def run(i, carry):
            step(lo + i * UNROLL, UNROLL, lo + (i - 1) * UNROLL, UNROLL)
            return carry

        lax.fori_loop(1, blocks, run, 0)
        x = lo + blocks * UNROLL
        if rest:
            step(x, rest, x - UNROLL, UNROLL)
            if after is not None:
                for store in after(x, rest):
                    store()
        elif after is not None:
            for store in after(x - UNROLL, UNROLL):
                store()

    src = u_ref
    for order in range(DEG - 1, 0, -1):
        dst = a_ref if src is not a_ref else b_ref

        def body(x, count, before, order=order, src=src, dst=dst):
            rows = [[src[x + r, g] for g in range(groups + 1)] for r in range(-1, count + 1)]
            sums = [[y_ref[x + r, g] for g in range(groups + 1)] for r in range(count)]
            starts = rows[1:-1] if order == DEG - 1 else [[u_ref[x + r, g] for g in range(groups + 1)] for r in range(count)]
            pending = before() if before is not None else []
            coef = power[order]
            for r in range(count):
                c2, d, c2s, ds = (spread(which, x + r) for which in (COND2, DIAG, COND2_S, DIAG_S))
                for g in range(groups + 1):
                    cc, dd = (c2, d) if g < groups else (c2s, ds)
                    total = sums[r][g] + (rows[r][g] + rows[r + 2][g])
                    applied = dd * rows[r + 1][g] + cc * total
                    if order == DEG - 1:
                        applied = power[DEG] * applied
                    dst[x + r, g] = coef * starts[r][g] + applied
            for store in pending:
                store()

        def after(x, count, dst=dst):
            rows = [[dst[x + r, g] for g in range(groups + 1)] for r in range(count)]
            stores = []
            for r in range(count):
                for g, total in enumerate(across(rows[r])):
                    def put(r=r, g=g, total=total):
                        y_ref[x + r, g] = total

                    stores.append(put)
            return stores

        swept(DEG - order, body, after)
        src = dst

    def last(x, count, before):
        rows = [[src[x + r, g] for g in range(groups)] for r in range(-1, count + 1)]
        for r in range(count):
            at = x + r - DEG
            cond, d, inverse = (spread(which, x + r) for which in (COND, DIAG, INVERSE))
            out = []
            for g in range(groups):
                total = y_ref[x + r, g] + (rows[r][g] + rows[r + 2][g])
                value = inverse * (power[0] * u_ref[x + r, g] + d * rows[r + 1][g]) + cond * total
                smooth_ref[pl.ds(g * SUB * width_x + at, SUB, stride=width_x), :] = value
                out.append(value)
            column = at * LANES if isinstance(at, int) else pl.multiple_of(at * LANES, LANES)
            for g in range(0, groups, 2):
                both = jnp.concatenate(out[g : g + 2], axis=0)
                low_ref[pl.ds(g * SUB, 2 * SUB), pl.ds(column, LANES)] = both.astype(BF16)

    swept(DEG, last)


def vmem():
    return pl.BlockSpec(memory_space=pltpu.VMEM)


def hbm():
    return pl.BlockSpec(memory_space=pltpu.HBM)


def filtered(adjoint, cell_ids, mat_diag, mat_cond, cheb_coef):
    cols, width_x, width_y = adjoint.shape
    groups = cols // SUB
    assert width_y == LANES and width_x % SUB == 0 and width_x >= DEG
    assert cols % SIDE == 0 and groups * SIDE <= LANES
    size_x = lax.axis_size("sx")
    size_y = lax.axis_size("sy")
    flat = adjoint.reshape(cols * width_x, width_y)
    n_kinds = 2 if size_y > 2 else 1
    row_shape = jax.ShapeDtypeStruct((DEG * groups + 1, SUB, LANES), F32)
    strip_shape = jax.ShapeDtypeStruct((width_x + width_x // SUB, SUB, LANES), F32)
    corner_shape = jax.ShapeDtypeStruct((DEG + 1, SUB, LANES), F32)
    small = [pltpu.SMEM(v.shape, F32) for v in (mat_diag, mat_cond, cheb_coef)]
    flat, ids, params, *packed = pl.pallas_call(
        functools.partial(pack_kernel, groups, width_x, n_kinds),
        out_shape=[
            jax.ShapeDtypeStruct(flat.shape, F32),
            jax.ShapeDtypeStruct(cell_ids.shape, jnp.int32),
            jax.ShapeDtypeStruct((3, SUB, LANES), F32),
        ]
        + [row_shape] * 2
        + [strip_shape, corner_shape, corner_shape] * n_kinds,
        in_specs=[hbm()] * 5,
        out_specs=[vmem()] * (5 + 3 * n_kinds),
        scratch_shapes=small + [pltpu.SemaphoreType.DMA((5,))],
        compiler_params=pltpu.CompilerParams(vmem_limit_bytes=VMEM_GRANT),
        name="pack",
    )(*(pltpu.with_memory_space_constraint(v, pltpu.HBM) for v in (flat, cell_ids, mat_diag, mat_cond, cheb_coef)))

    def swap(value, kind_x, kind_y):
        pairs = pairing(kind_x, kind_y, size_x, size_y)
        if not pairs:
            return jnp.zeros_like(value)
        return lax.ppermute(value, ("sx", "sy"), pairs)

    odd = swap(packed[1], 1, None)
    even = swap(packed[0], 0, None)
    strips = []
    for kind in range(n_kinds):
        strips.append(
            (
                swap(packed[2 + 3 * kind], None, kind),
                swap(packed[3 + 3 * kind], 0, kind),
                swap(packed[4 + 3 * kind], 1, kind),
            )
        )
    strip, strip_even, strip_odd = (functools.reduce(jnp.add, part) for part in zip(*strips))
    tall = width_x + 2 * DEG
    n_chunks = CHUNKS if groups % (2 * CHUNKS) == 0 else 1
    part = groups // n_chunks
    field = pltpu.VMEM((tall, part + 1, SUB, LANES), F32)
    smooth = []
    low = []
    for chunk in range(n_chunks):
        out_shape = [
            pltpu.VMEM((part * SUB * width_x, width_y), F32),
            pltpu.VMEM((part * SUB, width_x * width_y), BF16),
        ]
        scratch = [field] * 4 + [pltpu.VMEM((DEG + 1, SUB, LANES), F32)]
        operands = [params, flat, ids, even, odd, strip, strip_even, strip_odd]
        in_specs = [vmem()] * 8
        if chunk == 0:
            out_shape += [pltpu.VMEM((7, tall, LANES), F32)]
        else:
            operands += [table]
            in_specs += [vmem()]
        call = pl.pallas_call(
            functools.partial(filter_kernel, part, groups, chunk * part, width_x, chunk == 0),
            out_shape=out_shape,
            in_specs=in_specs,
            out_specs=[vmem()] * len(out_shape),
            scratch_shapes=scratch,
            compiler_params=pltpu.CompilerParams(vmem_limit_bytes=VMEM_GRANT),
            cost_estimate=pl.CostEstimate(flops=part * 3000000, bytes_accessed=part * 200000, transcendentals=0),
        )
        got = call(*operands)
        smooth.append(got[0])
        low.append(got[1])
        if chunk == 0:
            table = got[2]
    smooth = smooth[0] if n_chunks == 1 else jnp.concatenate(smooth)
    return smooth.reshape(adjoint.shape), low


def ring_order(size):
    return [0] + list(range(1, size, 2)) + list(range(2, size, 2))[::-1]


def stepped(before, me, steps):
    found = jnp.int32(0)
    for start in range(len(before)):
        spot = start
        for _ in range(steps):
            spot = before[spot]
        found = jnp.where(me == start, spot, found)
    return found


def gathered_product(low, rows):
    size = lax.axis_size("cr")
    order = ring_order(size)
    me = lax.axis_index("cr")
    hop = [(order[i], order[(i + 1) % size]) for i in range(size)] if size > 1 else []
    before = [0] * size
    for a, b in hop:
        before[b] = a
    pieces = list(low)
    whole = jnp.zeros((size, sum(p.shape[0] for p in pieces), rows.shape[0]), F32)
    for step in range(size):
        following = []
        if step < size - 1:
            for piece in pieces:
                following.append(lax.ppermute(piece, "cr", hop))
        piece = pieces[0] if len(pieces) == 1 else jnp.concatenate(pieces)
        product = lax.dot_general(piece, rows, (((1,), (1,)), ((), ())), preferred_element_type=F32)
        whole = lax.dynamic_update_slice(whole, product[None], (stepped(before, me, step), 0, 0))
        pieces = following
    return whole


def reduced(whole):
    size, cols, n_rows = whole.shape
    size_x = lax.axis_size("sx")
    size_y = lax.axis_size("sy")
    plane = size_x * size_y
    share = size * cols // plane
    whole = whole.reshape(size_x // 2, 2, size_y, share, n_rows)
    core = lax.axis_index("sx") % 2
    keep = lax.dynamic_index_in_dim(whole, core, 1, keepdims=False)
    send = lax.dynamic_index_in_dim(whole, 1 - core, 1, keepdims=False).astype(BF16)
    half = pairing(0, None, size_x, size_y)
    total = keep + lax.ppermute(send, ("sx", "sy"), half).astype(F32)
    total = total.reshape(plane // 2, share, n_rows)
    sy = lax.axis_index("sy")
    spot = (lax.axis_index("sx") // 2) * size_y + sy
    mine = lax.dynamic_index_in_dim(total, spot, 0, keepdims=False)
    arrived = []
    for shift in range(1, plane // 2):
        pairs = []
        for i in range(size_x):
            for j in range(size_y):
                other = ((i // 2) * size_y + j) ^ shift
                pairs.append((i * size_y + j, ((other // size_y) * 2 + i % 2) * size_y + other % size_y))
        out = lax.dynamic_index_in_dim(total, spot ^ shift, 0, keepdims=False).astype(BF16)
        arrived.append(lax.ppermute(out, ("sx", "sy"), pairs))
    for part in arrived:
        mine = mine + part.astype(F32)
    return mine.T


def on_device(adjoint, sensor_rows, cell_ids, mat_diag, mat_cond, cheb_coef):
    smoothed, low = filtered(adjoint, cell_ids, mat_diag, mat_cond, cheb_coef)
    rows = sensor_rows.reshape(sensor_rows.shape[0], -1)
    return smoothed, reduced(gathered_product(low, rows))


def solution(mesh):
    placed = (P("cr", "sx", "sy"), P("cr", "sx", "sy"), P("sx", "sy"), P(), P(), P())
    return jax.shard_map(
        on_device,
        mesh=mesh,
        in_specs=placed,
        out_specs=(P("cr", "sx", "sy"), P("cr", ("sx", "sy"))),
        check_vma=False,
    )
```

```python
import functools

import jax
import jax.numpy as jnp
from jax import lax
from jax.experimental import pallas as pl
from jax.experimental.pallas import tpu as pltpu
from jax.sharding import PartitionSpec as P


DEG = 8
SUB = 8
LANES = 128
SIDE = 2 * DEG
UNROLL = 8
CHUNKS = 2
VMEM_GRANT = 16 * 1024 * 1024
F32 = jnp.float32
BF16 = jnp.bfloat16


def partner(i, odd, size):
    j = i ^ 1 if not odd else ((i + 1) ^ 1) - 1
    return j if 0 <= j < size else None


def pairing(kind_x, kind_y, size_x, size_y):
    pairs = []
    for i in range(size_x):
        for j in range(size_y):
            a = i if kind_x is None else partner(i, kind_x, size_x)
            b = j if kind_y is None else partner(j, kind_y, size_y)
            if a is not None and b is not None:
                pairs.append((i * size_y + j, a * size_y + b))
    return pairs


def edge_lanes():
    place = lax.broadcasted_iota(jnp.int32, (SUB, LANES), 1) & (SIDE - 1)
    return jnp.where(place < DEG, DEG - 1 - place, LANES - 1 + DEG - place)


def lane_gather(tile, index):
    return jnp.take_along_axis(tile, index, axis=1, mode="promise_in_bounds")


def is_even(axis):
    return lax.axis_index(axis) % 2 == 0


def pack_kernel(groups, width_x, n_kinds, *refs):
    adj_hbm, ids_hbm, diag_hbm, cond_hbm, coef_hbm, adj_ref, ids_ref, params_ref = refs[:8]
    diag_ref, cond_ref, coef_ref, sem = refs[-4:]
    row_refs = refs[8:10]
    strip_refs = refs[10:-4]
    pairs = ((adj_hbm, adj_ref), (ids_hbm, ids_ref), (diag_hbm, diag_ref), (cond_hbm, cond_ref), (coef_hbm, coef_ref))
    copies = [pltpu.make_async_copy(src, dst, sem.at[i]) for i, (src, dst) in enumerate(pairs)]
    for copy in copies:
        copy.start()
    for copy in copies:
        copy.wait()
    upper_x = jnp.where(is_even("sx"), 1, 0)
    upper_y = jnp.where(is_even("sy"), 1, 0)
    index = edge_lanes()
    lane = lax.broadcasted_iota(jnp.int32, (SUB, LANES), 1)
    low_side = jnp.where((lane & (SIDE - 1)) < DEG, 1, 0)
    for which in range(2):
        upper = upper_x if which == 0 else 1 - upper_x
        base = pl.multiple_of(upper * (width_x - DEG), SUB)
        for row in range(DEG):
            for g in range(groups):
                row_refs[which][row * groups + g] = adj_ref[pl.ds(g * SUB * width_x + base + row, SUB, stride=width_x), :]
        row_refs[which][DEG * groups] = ids_ref[pl.ds(base, SUB), :].astype(F32) + 1.0
    for kind in range(n_kinds):
        upper = upper_y if kind == 0 else 1 - upper_y
        keep = (low_side ^ upper) == 1
        for row in range(width_x):
            strip = jnp.zeros((SUB, LANES), F32)
            for g in range(groups):
                tile = adj_ref[pl.ds(g * SUB * width_x + row, SUB, stride=width_x), :]
                strip = jnp.where((lane // SIDE) == g, lane_gather(tile, index), strip)
            strip_refs[2 * kind][row] = jnp.where(keep, strip, 0.0)
        for tile_x in range(width_x // SUB):
            ids = ids_ref[tile_x * SUB : (tile_x + 1) * SUB, :].astype(F32) + 1.0
            strip_refs[2 * kind][width_x + tile_x] = jnp.where(keep, lane_gather(ids, index), 0.0)
        for which in range(2):
            upper = upper_x if which == 0 else 1 - upper_x
            base = upper * (width_x - DEG)
            to, at = (row_refs[0], DEG * groups + 1 + kind * (DEG + 1)) if which == 0 else (strip_refs[2 * kind + 1], 0)
            for row in range(DEG):
                to[at + row] = strip_refs[2 * kind][base + row]
            to[at + DEG] = strip_refs[2 * kind][width_x + upper * (width_x // SUB - 1)]
    for i, ref in enumerate((diag_ref, cond_ref)):
        tile = jnp.zeros((SUB, LANES), F32)
        for m in range(ref.shape[0]):
            tile = jnp.where(lane == m + 1, ref[m], tile)
        params_ref[i] = tile
    tile = jnp.zeros((SUB, LANES), F32)
    for k, terms in enumerate(power_terms()):
        parts = [coef_ref[j] * float(t) for j, t in enumerate(terms) if t]
        tile = jnp.where(lane == k, functools.reduce(lambda p, q: p + q, parts), tile)
    params_ref[2] = tile


def power_terms():
    polys = [[1], [0, 1]]
    for _ in range(2, DEG + 1):
        doubled = [0] + [2 * t for t in polys[-1]]
        older = polys[-2] + [0] * (len(doubled) - len(polys[-2]))
        polys.append([p - q for p, q in zip(doubled, older)])
    return [[p[k] if k < len(p) else 0 for p in polys] for k in range(DEG + 1)]


COND, COND2, DIAG, COND_S, COND2_S, DIAG_S, INVERSE = range(7)


def filter_kernel(groups, all_groups, offset, width_x, first, *refs):
    params_ref, adj_ref, ids_ref, even_ref, odd_ref, strip_ref, strip_odd_ref = refs[:7]
    if first:
        smooth_ref, low_ref, table = refs[7:10]
    else:
        table, smooth_ref, low_ref = refs[7:10]
    u_ref, a_ref, b_ref, y_ref, power = refs[10:]
    tall = width_x + 2 * DEG
    beyond = width_x + width_x // SUB
    lane = lax.broadcasted_iota(jnp.int32, (SUB, LANES), 1)
    even_x = is_even("sx")
    for k in range(DEG + 1):
        power[k] = lane_gather(params_ref[2], jnp.full((SUB, LANES), k, jnp.int32))

    def lookup(ids, x0, strip):
        ids = ids.astype(jnp.int32)
        cond = lane_gather(params_ref[1], ids)
        table[COND_S if strip else COND, x0 : x0 + SUB, :] = cond
        table[COND2_S if strip else COND2, x0 : x0 + SUB, :] = cond * cond
        table[DIAG_S if strip else DIAG, x0 : x0 + SUB, :] = lane_gather(params_ref[0], ids)
        return cond

    def spread(which, x):
        return table[which, pl.ds(x, SUB, stride=0), :]

    first_lane = lane == 0
    last_lane = lane == LANES - 1
    place = lane & (SIDE - 1)
    at_high = place == DEG - 1
    at_low = place == DEG
    junction = lane // SIDE

    def across(tiles):
        sums = []
        meet = None
        strip = tiles[groups]
        for g, tile in enumerate(tiles[:groups]):
            off = (offset + g) * SIDE + DEG
            edge = pltpu.roll(strip, LANES - off, 1)
            left = jnp.where(first_lane, edge, pltpu.roll(tile, 1, 1))
            right = jnp.where(last_lane, edge, pltpu.roll(tile, LANES - 1, 1))
            sums.append(left + right)
            moved = pltpu.roll(tile, off, 1)
            meet = moved if meet is None else jnp.where(junction == offset + g, moved, meet)
        up = jnp.where(at_high, meet, pltpu.roll(strip, LANES - 1, 1))
        down = jnp.where(at_low, meet, pltpu.roll(strip, 1, 1))
        sums.append(up + down)
        return sums

    def place_row(x, tiles):
        for g in range(groups + 1):
            u_ref[x, g] = tiles[g]
        for g, total in enumerate(across(tiles)):
            y_ref[x, g] = total

    repeat = lane & (SIDE - 1)
    if first:
        for high in (False, True):
            x0 = tall - DEG if high else 0
            from_even = even_x if high else jnp.logical_not(even_x)
            lookup(jnp.where(from_even, even_ref[DEG * all_groups], odd_ref[DEG * all_groups]), x0, False)
            ids = jnp.where(from_even, strip_ref[beyond + DEG], strip_odd_ref[DEG])
            lookup(lane_gather(ids, repeat), x0, True)
        for tile_x in range(width_x // SUB):
            x0 = DEG + tile_x * SUB
            cond = lookup(ids_ref[tile_x * SUB : (tile_x + 1) * SUB, :] + 1, x0, False)
            table[INVERSE, x0 : x0 + SUB, :] = 1.0 / cond
            lookup(lane_gather(strip_ref[width_x + tile_x], repeat), x0, True)
    for high in (False, True):
        x0 = tall - DEG if high else 0
        from_even = even_x if high else jnp.logical_not(even_x)
        for row in range(DEG):
            scale = spread(COND, x0 + row)
            tiles = []
            for g in range(groups):
                at = row * all_groups + offset + g
                tiles.append(jnp.where(from_even, even_ref[at], odd_ref[at]) * scale)
            strip = jnp.where(from_even, strip_ref[beyond + row], strip_odd_ref[row])
            place_row(x0 + row, tiles + [strip * spread(COND_S, x0 + row)])
    for row in range(width_x):
        x = DEG + row
        scale = spread(COND, x)
        tiles = []
        for g in range(groups):
            tiles.append(adj_ref[pl.ds((offset + g) * SUB * width_x + row, SUB, stride=width_x), :] * scale)
        place_row(x, tiles + [strip_ref[row] * spread(COND_S, x)])

    def swept(lo, body, after=None):
        n = tall - 2 * lo
        blocks = n // UNROLL
        rest = n % UNROLL

        def step(x, count, x_before, count_before):
            body(x, count, None if after is None or not count_before else lambda: after(x_before, count_before))

        step(lo, UNROLL, None, 0)

        def run(i, carry):
            step(lo + i * UNROLL, UNROLL, lo + (i - 1) * UNROLL, UNROLL)
            return carry

        lax.fori_loop(1, blocks, run, 0)
        x = lo + blocks * UNROLL
        if rest:
            step(x, rest, x - UNROLL, UNROLL)
            if after is not None:
                for store in after(x, rest):
                    store()
        elif after is not None:
            for store in after(x - UNROLL, UNROLL):
                store()

    src = u_ref
    for order in range(DEG - 1, 0, -1):
        dst = a_ref if src is not a_ref else b_ref

        def body(x, count, before, order=order, src=src, dst=dst):
            rows = [[src[x + r, g] for g in range(groups + 1)] for r in range(-1, count + 1)]
            sums = [[y_ref[x + r, g] for g in range(groups + 1)] for r in range(count)]
            starts = rows[1:-1] if order == DEG - 1 else [[u_ref[x + r, g] for g in range(groups + 1)] for r in range(count)]
            pending = before() if before is not None else []
            coef = power[order]
            for r in range(count):
                c2, d, c2s, ds = (spread(which, x + r) for which in (COND2, DIAG, COND2_S, DIAG_S))
                for g in range(groups + 1):
                    cc, dd = (c2, d) if g < groups else (c2s, ds)
                    total = sums[r][g] + (rows[r][g] + rows[r + 2][g])
                    applied = dd * rows[r + 1][g] + cc * total
                    if order == DEG - 1:
                        applied = power[DEG] * applied
                    dst[x + r, g] = coef * starts[r][g] + applied
            for store in pending:
                store()

        def after(x, count, dst=dst):
            rows = [[dst[x + r, g] for g in range(groups + 1)] for r in range(count)]
            stores = []
            for r in range(count):
                for g, total in enumerate(across(rows[r])):
                    def put(r=r, g=g, total=total):
                        y_ref[x + r, g] = total

                    stores.append(put)
            return stores

        swept(DEG - order, body, after)
        src = dst

    def last(x, count, before):
        rows = [[src[x + r, g] for g in range(groups)] for r in range(-1, count + 1)]
        for r in range(count):
            at = x + r - DEG
            cond, d, inverse = (spread(which, x + r) for which in (COND, DIAG, INVERSE))
            out = []
            for g in range(groups):
                total = y_ref[x + r, g] + (rows[r][g] + rows[r + 2][g])
                value = inverse * (power[0] * u_ref[x + r, g] + d * rows[r + 1][g]) + cond * total
                smooth_ref[pl.ds(g * SUB * width_x + at, SUB, stride=width_x), :] = value
                out.append(value)
            column = at * LANES if isinstance(at, int) else pl.multiple_of(at * LANES, LANES)
            for g in range(0, groups, 2):
                both = jnp.concatenate(out[g : g + 2], axis=0)
                low_ref[pl.ds(g * SUB, 2 * SUB), pl.ds(column, LANES)] = both.astype(BF16)

    swept(DEG, last)


def vmem():
    return pl.BlockSpec(memory_space=pltpu.VMEM)


def hbm():
    return pl.BlockSpec(memory_space=pltpu.HBM)


def filtered(adjoint, cell_ids, mat_diag, mat_cond, cheb_coef):
    cols, width_x, width_y = adjoint.shape
    groups = cols // SUB
    assert width_y == LANES and width_x % SUB == 0 and width_x >= DEG
    assert cols % SIDE == 0 and groups * SIDE <= LANES
    size_x = lax.axis_size("sx")
    size_y = lax.axis_size("sy")
    flat = adjoint.reshape(cols * width_x, width_y)
    n_kinds = 2 if size_y > 2 else 1
    row_tiles = DEG * groups + 1
    row_shapes = [
        jax.ShapeDtypeStruct((row_tiles + n_kinds * (DEG + 1), SUB, LANES), F32),
        jax.ShapeDtypeStruct((row_tiles, SUB, LANES), F32),
    ]
    strip_shape = jax.ShapeDtypeStruct((width_x + width_x // SUB, SUB, LANES), F32)
    corner_shape = jax.ShapeDtypeStruct((DEG + 1, SUB, LANES), F32)
    small = [pltpu.SMEM(v.shape, F32) for v in (mat_diag, mat_cond, cheb_coef)]
    flat, ids, params, *packed = pl.pallas_call(
        functools.partial(pack_kernel, groups, width_x, n_kinds),
        out_shape=[
            jax.ShapeDtypeStruct(flat.shape, F32),
            jax.ShapeDtypeStruct(cell_ids.shape, jnp.int32),
            jax.ShapeDtypeStruct((3, SUB, LANES), F32),
        ]
        + row_shapes
        + [strip_shape, corner_shape] * n_kinds,
        in_specs=[hbm()] * 5,
        out_specs=[vmem()] * (5 + 2 * n_kinds),
        scratch_shapes=small + [pltpu.SemaphoreType.DMA((5,))],
        compiler_params=pltpu.CompilerParams(vmem_limit_bytes=VMEM_GRANT),
        name="pack",
    )(*(pltpu.with_memory_space_constraint(v, pltpu.HBM) for v in (flat, cell_ids, mat_diag, mat_cond, cheb_coef)))

    def swap(value, kind_x, kind_y):
        pairs = pairing(kind_x, kind_y, size_x, size_y)
        if not pairs:
            return jnp.zeros_like(value)
        return lax.ppermute(value, ("sx", "sy"), pairs)

    even = swap(packed[0], 0, None)
    odd = swap(packed[1], 1, None)
    strips = []
    for kind in range(n_kinds):
        corner = swap(packed[3 + 2 * kind], 1, kind)
        start = row_tiles + kind * (DEG + 1)
        tall_strip = jnp.concatenate([packed[2 + 2 * kind], even[start : start + DEG + 1]])
        strips.append((swap(tall_strip, None, kind), corner))
    strip, strip_odd = (functools.reduce(jnp.add, part) for part in zip(*strips))
    tall = width_x + 2 * DEG
    n_chunks = CHUNKS if groups % (2 * CHUNKS) == 0 else 1
    part = groups // n_chunks
    field = pltpu.VMEM((tall, part + 1, SUB, LANES), F32)
    smooth = []
    low = []
    for chunk in range(n_chunks):
        out_shape = [
            pltpu.VMEM((part * SUB * width_x, width_y), F32),
            pltpu.VMEM((part * SUB, width_x * width_y), BF16),
        ]
        scratch = [field] * 4 + [pltpu.VMEM((DEG + 1, SUB, LANES), F32)]
        operands = [params, flat, ids, even, odd, strip, strip_odd]
        in_specs = [vmem()] * 7
        if chunk == 0:
            out_shape += [pltpu.VMEM((7, tall, LANES), F32)]
        else:
            operands += [table]
            in_specs += [vmem()]
        call = pl.pallas_call(
            functools.partial(filter_kernel, part, groups, chunk * part, width_x, chunk == 0),
            out_shape=out_shape,
            in_specs=in_specs,
            out_specs=[vmem()] * len(out_shape),
            scratch_shapes=scratch,
            compiler_params=pltpu.CompilerParams(vmem_limit_bytes=VMEM_GRANT),
            cost_estimate=pl.CostEstimate(flops=part * 3000000, bytes_accessed=part * 200000, transcendentals=0),
        )
        got = call(*operands)
        smooth.append(got[0])
        low.append(got[1])
        if chunk == 0:
            table = got[2]
    smooth = smooth[0] if n_chunks == 1 else jnp.concatenate(smooth)
    return smooth.reshape(adjoint.shape), low


def ring_order(size):
    return [0] + list(range(1, size, 2)) + list(range(2, size, 2))[::-1]


def stepped(before, me, steps):
    found = jnp.int32(0)
    for start in range(len(before)):
        spot = start
        for _ in range(steps):
            spot = before[spot]
        found = jnp.where(me == start, spot, found)
    return found


def gathered_product(low, rows):
    size = lax.axis_size("cr")
    order = ring_order(size)
    me = lax.axis_index("cr")
    hop = [(order[i], order[(i + 1) % size]) for i in range(size)] if size > 1 else []
    before = [0] * size
    for a, b in hop:
        before[b] = a
    pieces = list(low)
    whole = jnp.zeros((size, sum(p.shape[0] for p in pieces), rows.shape[0]), F32)
    for step in range(size):
        following = []
        if step < size - 1:
            for piece in pieces:
                following.append(lax.ppermute(piece, "cr", hop))
        piece = pieces[0] if len(pieces) == 1 else jnp.concatenate(pieces)
        product = lax.dot_general(piece, rows, (((1,), (1,)), ((), ())), preferred_element_type=F32)
        whole = lax.dynamic_update_slice(whole, product[None], (stepped(before, me, step), 0, 0))
        pieces = following
    return whole


def reduced(whole):
    size, cols, n_rows = whole.shape
    size_x = lax.axis_size("sx")
    size_y = lax.axis_size("sy")
    plane = size_x * size_y
    share = size * cols // plane
    whole = whole.reshape(size_x // 2, 2, size_y, share, n_rows)
    core = lax.axis_index("sx") % 2
    keep = lax.dynamic_index_in_dim(whole, core, 1, keepdims=False)
    send = lax.dynamic_index_in_dim(whole, 1 - core, 1, keepdims=False).astype(BF16)
    half = pairing(0, None, size_x, size_y)
    total = keep + lax.ppermute(send, ("sx", "sy"), half).astype(F32)
    total = total.reshape(plane // 2, share, n_rows)
    sy = lax.axis_index("sy")
    spot = (lax.axis_index("sx") // 2) * size_y + sy
    mine = lax.dynamic_index_in_dim(total, spot, 0, keepdims=False)
    arrived = []
    for shift in range(1, plane // 2):
        pairs = []
        for i in range(size_x):
            for j in range(size_y):
                other = ((i // 2) * size_y + j) ^ shift
                pairs.append((i * size_y + j, ((other // size_y) * 2 + i % 2) * size_y + other % size_y))
        out = lax.dynamic_index_in_dim(total, spot ^ shift, 0, keepdims=False).astype(BF16)
        arrived.append(lax.ppermute(out, ("sx", "sy"), pairs))
    for part in arrived:
        mine = mine + part.astype(F32)
    return mine.T


def on_device(adjoint, sensor_rows, cell_ids, mat_diag, mat_cond, cheb_coef):
    smoothed, low = filtered(adjoint, cell_ids, mat_diag, mat_cond, cheb_coef)
    rows = sensor_rows.reshape(sensor_rows.shape[0], -1)
    return smoothed, reduced(gathered_product(low, rows))


def solution(mesh):
    placed = (P("cr", "sx", "sy"), P("cr", "sx", "sy"), P("sx", "sy"), P(), P(), P())
    return jax.shard_map(
        on_device,
        mesh=mesh,
        in_specs=placed,
        out_specs=(P("cr", "sx", "sy"), P("cr", ("sx", "sy"))),
        check_vma=False,
    )
```

```python
import functools

import jax
import jax.numpy as jnp
from jax import lax
from jax.experimental import pallas as pl
from jax.experimental.pallas import tpu as pltpu
from jax.sharding import PartitionSpec as P


DEG = 8
SUB = 8
LANES = 128
SIDE = 2 * DEG
UNROLL = 8
SHARES = (1, 1)
VMEM_GRANT = 16 * 1024 * 1024
F32 = jnp.float32
BF16 = jnp.bfloat16


def partner(i, odd, size):
    j = i ^ 1 if not odd else ((i + 1) ^ 1) - 1
    return j if 0 <= j < size else None


def pairing(kind_x, kind_y, size_x, size_y):
    pairs = []
    for i in range(size_x):
        for j in range(size_y):
            a = i if kind_x is None else partner(i, kind_x, size_x)
            b = j if kind_y is None else partner(j, kind_y, size_y)
            if a is not None and b is not None:
                pairs.append((i * size_y + j, a * size_y + b))
    return pairs


def edge_lanes():
    place = lax.broadcasted_iota(jnp.int32, (SUB, LANES), 1) & (SIDE - 1)
    return jnp.where(place < DEG, DEG - 1 - place, LANES - 1 + DEG - place)


def lane_gather(tile, index):
    return jnp.take_along_axis(tile, index, axis=1, mode="promise_in_bounds")


def is_even(axis):
    return lax.axis_index(axis) % 2 == 0


def pack_kernel(groups, width_x, n_kinds, *refs):
    adj_hbm, ids_hbm, diag_hbm, cond_hbm, coef_hbm, adj_ref, ids_ref, params_ref = refs[:8]
    diag_ref, cond_ref, coef_ref, sem = refs[-4:]
    row_refs = refs[8:10]
    strip_refs = refs[10:-4]
    pairs = ((adj_hbm, adj_ref), (ids_hbm, ids_ref), (diag_hbm, diag_ref), (cond_hbm, cond_ref), (coef_hbm, coef_ref))
    copies = [pltpu.make_async_copy(src, dst, sem.at[i]) for i, (src, dst) in enumerate(pairs)]
    for copy in copies:
        copy.start()
    for copy in copies:
        copy.wait()
    upper_x = jnp.where(is_even("sx"), 1, 0)
    upper_y = jnp.where(is_even("sy"), 1, 0)
    index = edge_lanes()
    lane = lax.broadcasted_iota(jnp.int32, (SUB, LANES), 1)
    low_side = jnp.where((lane & (SIDE - 1)) < DEG, 1, 0)
    for which in range(2):
        upper = upper_x if which == 0 else 1 - upper_x
        base = pl.multiple_of(upper * (width_x - DEG), SUB)
        for row in range(DEG):
            for g in range(groups):
                tile = adj_ref[pl.ds(g * SUB * width_x + base + row, SUB, stride=width_x), :]
                row_refs[which][row * groups + g] = tile.astype(BF16)
        row_refs[which][DEG * groups] = (ids_ref[pl.ds(base, SUB), :].astype(F32) + 1.0).astype(BF16)
    for kind in range(n_kinds):
        upper = upper_y if kind == 0 else 1 - upper_y
        keep = (low_side ^ upper) == 1
        for row in range(width_x):
            strip = jnp.zeros((SUB, LANES), F32)
            for g in range(groups):
                tile = adj_ref[pl.ds(g * SUB * width_x + row, SUB, stride=width_x), :]
                strip = jnp.where((lane // SIDE) == g, lane_gather(tile, index), strip)
            strip_refs[2 * kind][row] = jnp.where(keep, strip, 0.0).astype(BF16)
        for tile_x in range(width_x // SUB):
            ids = ids_ref[tile_x * SUB : (tile_x + 1) * SUB, :].astype(F32) + 1.0
            strip_refs[2 * kind][width_x + tile_x] = jnp.where(keep, lane_gather(ids, index), 0.0).astype(BF16)
        for which in range(2):
            upper = upper_x if which == 0 else 1 - upper_x
            base = upper * (width_x - DEG)
            to, at = (row_refs[0], DEG * groups + 1 + kind * (DEG + 1)) if which == 0 else (strip_refs[2 * kind + 1], 0)
            for row in range(DEG):
                to[at + row] = strip_refs[2 * kind][base + row]
            to[at + DEG] = strip_refs[2 * kind][width_x + upper * (width_x // SUB - 1)]
    for i, ref in enumerate((diag_ref, cond_ref)):
        tile = jnp.zeros((SUB, LANES), F32)
        for m in range(ref.shape[0]):
            tile = jnp.where(lane == m + 1, ref[m], tile)
        params_ref[i] = tile
    tile = jnp.zeros((SUB, LANES), F32)
    for k, terms in enumerate(power_terms()):
        parts = [coef_ref[j] * float(t) for j, t in enumerate(terms) if t]
        tile = jnp.where(lane == k, functools.reduce(lambda p, q: p + q, parts), tile)
    params_ref[2] = tile


def power_terms():
    polys = [[1], [0, 1]]
    for _ in range(2, DEG + 1):
        doubled = [0] + [2 * t for t in polys[-1]]
        older = polys[-2] + [0] * (len(doubled) - len(polys[-2]))
        polys.append([p - q for p, q in zip(doubled, older)])
    return [[p[k] if k < len(p) else 0 for p in polys] for k in range(DEG + 1)]


COND, COND2, DIAG, COND_S, COND2_S, DIAG_S, INVERSE = range(7)


def filter_kernel(groups, all_groups, offset, width_x, first, *refs):
    params_ref, adj_ref, ids_ref, even_ref, odd_ref, strip_ref, strip_odd_ref = refs[:7]
    if first:
        smooth_ref, low_ref, table = refs[7:10]
    else:
        table, smooth_ref, low_ref = refs[7:10]
    u_ref, a_ref, b_ref, y_ref, power = refs[10:]
    tall = width_x + 2 * DEG
    beyond = width_x + width_x // SUB
    lane = lax.broadcasted_iota(jnp.int32, (SUB, LANES), 1)
    even_x = is_even("sx")
    for k in range(DEG + 1):
        power[k] = lane_gather(params_ref[2], jnp.full((SUB, LANES), k, jnp.int32))

    def lookup(ids, x0, strip):
        ids = ids.astype(jnp.int32)
        cond = lane_gather(params_ref[1], ids)
        table[COND_S if strip else COND, x0 : x0 + SUB, :] = cond
        table[COND2_S if strip else COND2, x0 : x0 + SUB, :] = cond * cond
        table[DIAG_S if strip else DIAG, x0 : x0 + SUB, :] = lane_gather(params_ref[0], ids)
        return cond

    def spread(which, x):
        return table[which, pl.ds(x, SUB, stride=0), :]

    first_lane = lane == 0
    last_lane = lane == LANES - 1
    place = lane & (SIDE - 1)
    at_high = place == DEG - 1
    at_low = place == DEG
    junction = lane // SIDE

    def across(tiles):
        sums = []
        meet = None
        strip = tiles[groups]
        for g, tile in enumerate(tiles[:groups]):
            off = (offset + g) * SIDE + DEG
            edge = pltpu.roll(strip, LANES - off, 1)
            left = jnp.where(first_lane, edge, pltpu.roll(tile, 1, 1))
            right = jnp.where(last_lane, edge, pltpu.roll(tile, LANES - 1, 1))
            sums.append(left + right)
            moved = pltpu.roll(tile, off, 1)
            meet = moved if meet is None else jnp.where(junction == offset + g, moved, meet)
        up = jnp.where(at_high, meet, pltpu.roll(strip, LANES - 1, 1))
        down = jnp.where(at_low, meet, pltpu.roll(strip, 1, 1))
        sums.append(up + down)
        return sums

    def place_row(x, tiles):
        for g in range(groups + 1):
            u_ref[x, g] = tiles[g]
        for g, total in enumerate(across(tiles)):
            y_ref[x, g] = total

    repeat = lane & (SIDE - 1)

    def pick(from_even, one, other):
        return jnp.where(from_even, one.astype(F32), other.astype(F32))

    if first:
        for high in (False, True):
            x0 = tall - DEG if high else 0
            from_even = even_x if high else jnp.logical_not(even_x)
            lookup(pick(from_even, even_ref[DEG * all_groups], odd_ref[DEG * all_groups]), x0, False)
            ids = pick(from_even, strip_ref[beyond + DEG], strip_odd_ref[DEG])
            lookup(lane_gather(ids, repeat), x0, True)
        for tile_x in range(width_x // SUB):
            x0 = DEG + tile_x * SUB
            cond = lookup(ids_ref[tile_x * SUB : (tile_x + 1) * SUB, :] + 1, x0, False)
            table[INVERSE, x0 : x0 + SUB, :] = 1.0 / cond
            lookup(lane_gather(strip_ref[width_x + tile_x].astype(F32), repeat), x0, True)
    for high in (False, True):
        x0 = tall - DEG if high else 0
        from_even = even_x if high else jnp.logical_not(even_x)
        for row in range(DEG):
            scale = spread(COND, x0 + row)
            tiles = []
            for g in range(groups):
                at = row * all_groups + offset + g
                tiles.append(pick(from_even, even_ref[at], odd_ref[at]) * scale)
            strip = pick(from_even, strip_ref[beyond + row], strip_odd_ref[row])
            place_row(x0 + row, tiles + [strip * spread(COND_S, x0 + row)])
    for row in range(width_x):
        x = DEG + row
        scale = spread(COND, x)
        tiles = []
        for g in range(groups):
            tiles.append(adj_ref[pl.ds((offset + g) * SUB * width_x + row, SUB, stride=width_x), :] * scale)
        place_row(x, tiles + [strip_ref[row].astype(F32) * spread(COND_S, x)])

    def swept(lo, body, after=None):
        n = tall - 2 * lo
        blocks = n // UNROLL
        rest = n % UNROLL

        def step(x, count, x_before, count_before):
            body(x, count, None if after is None or not count_before else lambda: after(x_before, count_before))

        step(lo, UNROLL, None, 0)

        for i in range(1, blocks):
            step(lo + i * UNROLL, UNROLL, lo + (i - 1) * UNROLL, UNROLL)
        x = lo + blocks * UNROLL
        if rest:
            step(x, rest, x - UNROLL, UNROLL)
            if after is not None:
                for store in after(x, rest):
                    store()
        elif after is not None:
            for store in after(x - UNROLL, UNROLL):
                store()

    src = u_ref
    for order in range(DEG - 1, 0, -1):
        dst = a_ref if src is not a_ref else b_ref

        def body(x, count, before, order=order, src=src, dst=dst):
            rows = [[src[x + r, g] for g in range(groups + 1)] for r in range(-1, count + 1)]
            sums = [[y_ref[x + r, g] for g in range(groups + 1)] for r in range(count)]
            starts = rows[1:-1] if order == DEG - 1 else [[u_ref[x + r, g] for g in range(groups + 1)] for r in range(count)]
            pending = before() if before is not None else []
            coef = power[order]
            for r in range(count):
                c2, d, c2s, ds = (spread(which, x + r) for which in (COND2, DIAG, COND2_S, DIAG_S))
                for g in range(groups + 1):
                    cc, dd = (c2, d) if g < groups else (c2s, ds)
                    total = sums[r][g] + (rows[r][g] + rows[r + 2][g])
                    applied = dd * rows[r + 1][g] + cc * total
                    if order == DEG - 1:
                        applied = power[DEG] * applied
                    dst[x + r, g] = coef * starts[r][g] + applied
            for store in pending:
                store()

        def after(x, count, dst=dst):
            rows = [[dst[x + r, g] for g in range(groups + 1)] for r in range(count)]
            stores = []
            for r in range(count):
                for g, total in enumerate(across(rows[r])):
                    def put(r=r, g=g, total=total):
                        y_ref[x + r, g] = total

                    stores.append(put)
            return stores

        swept(DEG - order, body, after)
        src = dst

    def last(x, count, before):
        rows = [[src[x + r, g] for g in range(groups)] for r in range(-1, count + 1)]
        for r in range(count):
            at = x + r - DEG
            cond, d, inverse = (spread(which, x + r) for which in (COND, DIAG, INVERSE))
            out = []
            for g in range(groups):
                total = y_ref[x + r, g] + (rows[r][g] + rows[r + 2][g])
                value = inverse * (power[0] * u_ref[x + r, g] + d * rows[r + 1][g]) + cond * total
                smooth_ref[pl.ds(g * SUB * width_x + at, SUB, stride=width_x), :] = value
                out.append(value)
            column = at * LANES
            for g in range(0, groups, 2):
                both = jnp.concatenate(out[g : g + 2], axis=0)
                low_ref[pl.ds(g * SUB, 2 * SUB), pl.ds(column, LANES)] = both.astype(BF16)

    swept(DEG, last)


def chunk_sizes(groups):
    unit = groups // sum(SHARES)
    if groups % sum(SHARES) or any(unit * share % 2 for share in SHARES):
        return (groups,)
    return tuple(unit * share for share in SHARES)


def vmem():
    return pl.BlockSpec(memory_space=pltpu.VMEM)


def hbm():
    return pl.BlockSpec(memory_space=pltpu.HBM)


def filtered(adjoint, cell_ids, mat_diag, mat_cond, cheb_coef):
    cols, width_x, width_y = adjoint.shape
    groups = cols // SUB
    assert width_y == LANES and width_x % SUB == 0 and width_x >= DEG
    assert cols % SIDE == 0 and groups * SIDE <= LANES
    size_x = lax.axis_size("sx")
    size_y = lax.axis_size("sy")
    flat = adjoint.reshape(cols * width_x, width_y)
    n_kinds = 2 if size_y > 2 else 1
    row_tiles = DEG * groups + 1
    row_shapes = [
        jax.ShapeDtypeStruct((row_tiles + n_kinds * (DEG + 1), SUB, LANES), BF16),
        jax.ShapeDtypeStruct((row_tiles, SUB, LANES), BF16),
    ]
    strip_shape = jax.ShapeDtypeStruct((width_x + width_x // SUB, SUB, LANES), BF16)
    corner_shape = jax.ShapeDtypeStruct((DEG + 1, SUB, LANES), BF16)
    small = [pltpu.SMEM(v.shape, F32) for v in (mat_diag, mat_cond, cheb_coef)]
    flat, ids, params, *packed = pl.pallas_call(
        functools.partial(pack_kernel, groups, width_x, n_kinds),
        out_shape=[
            jax.ShapeDtypeStruct(flat.shape, F32),
            jax.ShapeDtypeStruct(cell_ids.shape, jnp.int32),
            jax.ShapeDtypeStruct((3, SUB, LANES), F32),
        ]
        + row_shapes
        + [strip_shape, corner_shape] * n_kinds,
        in_specs=[hbm()] * 5,
        out_specs=[vmem()] * (5 + 2 * n_kinds),
        scratch_shapes=small + [pltpu.SemaphoreType.DMA((5,))],
        compiler_params=pltpu.CompilerParams(vmem_limit_bytes=VMEM_GRANT),
        name="pack",
    )(*(pltpu.with_memory_space_constraint(v, pltpu.HBM) for v in (flat, cell_ids, mat_diag, mat_cond, cheb_coef)))

    def swap(value, kind_x, kind_y):
        pairs = pairing(kind_x, kind_y, size_x, size_y)
        if not pairs:
            return jnp.zeros_like(value)
        return lax.ppermute(value, ("sx", "sy"), pairs)

    even = swap(packed[0], 0, None)
    odd = swap(packed[1], 1, None)
    strips = []
    for kind in range(n_kinds):
        corner = swap(packed[3 + 2 * kind], 1, kind)
        start = row_tiles + kind * (DEG + 1)
        tall_strip = jnp.concatenate([packed[2 + 2 * kind], even[start : start + DEG + 1]])
        strips.append((swap(tall_strip, None, kind), corner))
    strip, strip_odd = (functools.reduce(jnp.add, part) for part in zip(*strips))
    tall = width_x + 2 * DEG
    parts = chunk_sizes(groups)
    smooth = []
    low = []
    for chunk, part in enumerate(parts):
        field = pltpu.VMEM((tall, part + 1, SUB, LANES), F32)
        out_shape = [
            pltpu.VMEM((part * SUB * width_x, width_y), F32),
            pltpu.VMEM((part * SUB, width_x * width_y), BF16),
        ]
        scratch = [field] * 4 + [pltpu.VMEM((DEG + 1, SUB, LANES), F32)]
        operands = [params, flat, ids, even, odd, strip, strip_odd]
        in_specs = [vmem()] * 7
        if chunk == 0:
            out_shape += [pltpu.VMEM((7, tall, LANES), F32)]
        else:
            operands += [table]
            in_specs += [vmem()]
        call = pl.pallas_call(
            functools.partial(filter_kernel, part, groups, sum(parts[:chunk]), width_x, chunk == 0),
            out_shape=out_shape,
            in_specs=in_specs,
            out_specs=[vmem()] * len(out_shape),
            scratch_shapes=scratch,
            compiler_params=pltpu.CompilerParams(vmem_limit_bytes=VMEM_GRANT),
            cost_estimate=pl.CostEstimate(flops=part * 3000000, bytes_accessed=part * 200000, transcendentals=0),
        )
        got = call(*operands)
        smooth.append(got[0])
        low.append(got[1])
        if chunk == 0:
            table = got[2]
    smooth = smooth[0] if len(parts) == 1 else jnp.concatenate(smooth)
    return smooth.reshape(adjoint.shape), low


def ring_order(size):
    return [0] + list(range(1, size, 2)) + list(range(2, size, 2))[::-1]


def stepped(before, me, steps):
    found = jnp.int32(0)
    for start in range(len(before)):
        spot = start
        for _ in range(steps):
            spot = before[spot]
        found = jnp.where(me == start, spot, found)
    return found


def gathered_product(low, rows):
    size = lax.axis_size("cr")
    order = ring_order(size)
    me = lax.axis_index("cr")
    hop = [(order[i], order[(i + 1) % size]) for i in range(size)] if size > 1 else []
    before = [0] * size
    for a, b in hop:
        before[b] = a
    pieces = list(low)
    whole = jnp.zeros((size, sum(p.shape[0] for p in pieces), rows.shape[0]), F32)
    for step in range(size):
        following = []
        if step < size - 1:
            for piece in pieces:
                following.append(lax.ppermute(piece, "cr", hop))
        piece = pieces[0] if len(pieces) == 1 else jnp.concatenate(pieces)
        product = lax.dot_general(piece, rows, (((1,), (1,)), ((), ())), preferred_element_type=F32)
        whole = lax.dynamic_update_slice(whole, product[None], (stepped(before, me, step), 0, 0))
        pieces = following
    return whole


def reduced(whole):
    size, cols, n_rows = whole.shape
    size_x = lax.axis_size("sx")
    size_y = lax.axis_size("sy")
    plane = size_x * size_y
    share = size * cols // plane
    whole = whole.reshape(size_x // 2, 2, size_y, share, n_rows)
    core = lax.axis_index("sx") % 2
    keep = lax.dynamic_index_in_dim(whole, core, 1, keepdims=False)
    send = lax.dynamic_index_in_dim(whole, 1 - core, 1, keepdims=False).astype(BF16)
    half = pairing(0, None, size_x, size_y)
    total = keep + lax.ppermute(send, ("sx", "sy"), half).astype(F32)
    total = total.reshape(plane // 2, share, n_rows)
    sy = lax.axis_index("sy")
    spot = (lax.axis_index("sx") // 2) * size_y + sy
    mine = lax.dynamic_index_in_dim(total, spot, 0, keepdims=False)
    arrived = []
    for shift in range(1, plane // 2):
        pairs = []
        for i in range(size_x):
            for j in range(size_y):
                other = ((i // 2) * size_y + j) ^ shift
                pairs.append((i * size_y + j, ((other // size_y) * 2 + i % 2) * size_y + other % size_y))
        out = lax.dynamic_index_in_dim(total, spot ^ shift, 0, keepdims=False).astype(BF16)
        arrived.append(lax.ppermute(out, ("sx", "sy"), pairs))
    for part in arrived:
        mine = mine + part.astype(F32)
    return mine.T


def on_device(adjoint, sensor_rows, cell_ids, mat_diag, mat_cond, cheb_coef):
    smoothed, low = filtered(adjoint, cell_ids, mat_diag, mat_cond, cheb_coef)
    rows = sensor_rows.reshape(sensor_rows.shape[0], -1)
    return smoothed, reduced(gathered_product(low, rows))


def solution(mesh):
    placed = (P("cr", "sx", "sy"), P("cr", "sx", "sy"), P("sx", "sy"), P(), P(), P())
    return jax.shard_map(
        on_device,
        mesh=mesh,
        in_specs=placed,
        out_specs=(P("cr", "sx", "sy"), P("cr", ("sx", "sy"))),
        check_vma=False,
    )
```
